32 devices in a mesh: groups: 2 (over y), dp: 4 (over z), layer: 4 (over x, core).
Axes of the slice: x: 2, y: 2, z: 4, core: 2. Of those that a mesh axis runs over, the one named last changes fastest.
Arguments:
- layer_inputs: float32 [4, 1024, 512], P('layer', ('groups', 'dp')), parts along dimension 1, may hold values from -6 to 6
- pre_acts: float32 [4, 1024, 512], P('layer', ('groups', 'dp')), parts along dimension 1, may hold values from -6 to 6
- layer_outputs: float32 [4, 1024, 512], P('layer', ('groups', 'dp')), parts along dimension 1, may hold values from -6 to 6
- multipliers: float32 [4, 1024, 512], P('layer', ('groups', 'dp')), parts along dimension 1, may hold values from -6 to 6
- weights: float32 [8, 512, 512], P(('groups', 'layer')), parts along dimension 0, may hold values from -0.25 to 0.25
- biases: float32 [8, 512], P(('groups', 'layer')), parts along dimension 0, may hold values from -3 to 3
- prev_outputs: float32 [1024, 512], P(('groups', 'dp')), parts along dimension 0, may hold values from -6 to 6
- prev_multipliers: float32 [1024, 512], P(('groups', 'dp')), parts along dimension 0, may hold values from -6 to 6
- next_inputs: float32 [1024, 512], P(('groups', 'dp')), parts along dimension 0, may hold values from -6 to 6
- row_order: int32 [8, 128], P(('groups', 'dp')), parts along dimension 0, may hold values from 0 to 127, each once within a row
Outputs:
- new_inputs: float32 [4, 1024, 512], P('layer', ('groups', 'dp')), parts along dimension 1
- new_preacts: float32 [4, 1024, 512], P('layer', ('groups', 'dp')), parts along dimension 1
- new_outputs: float32 [4, 1024, 512], P('layer', ('groups', 'dp')), parts along dimension 1
- new_multipliers: float32 [4, 1024, 512], P('layer', ('groups', 'dp')), parts along dimension 1
- new_weights: float32 [8, 512, 512], P(('groups', 'layer')), parts along dimension 0
- new_biases: float32 [8, 512], P(('groups', 'layer')), parts along dimension 0
The draws below stay inside these ranges and needn't reach their ends.
There are 2 independent parts, one for each index of `groups`. The reference program is written for one: setup_inputs(seed, part) draws one part's arguments, and reference() takes and returns one part's arrays. A program takes and returns all parts, laid end to end along the dimension named above; each array names one. Nothing has to cross between parts.
Inputs may be any that keep to these rules, and one draw needn't show every extreme that they name: Each row of row_order holds every number of 0 to 127 once.
All inputs are finite; a program needn't handle non-finite values.
Results may differ from the reference program's by a relative error of at most 0.0001.
Values sent between devices are 32-bit elements; how exact they have to be, the bound alone decides.
A program may use at most 64 MiB of HBM per device.

```python
import jax
import jax.numpy as jnp
from jax import lax

D = 512
ROWS = 128
INNER = 3
PASSES = 1
NODES = 512
LAYERS = 4
N_DP = 4


def block_scale(stream_key, extent, cuts, least, largest):
    loudness = 1.0
    for position, shards_of in cuts:
        draws = jax.random.uniform(jax.random.fold_in(jax.random.fold_in(stream_key, 6), position), (shards_of,), jnp.float32, least / len(cuts), largest / len(cuts))
        loudness = loudness * jnp.repeat(jnp.exp(draws), extent[position] // shards_of).reshape((-1,) + (1,) * (len(extent) - 1 - position))
    return loudness


def gaussian(stream_key, shape, width, most, cuts=(), held_as=jnp.bfloat16):
    values = width * jax.random.normal(stream_key, shape, jnp.float32)
    if cuts:
        values = values * block_scale(stream_key, shape, cuts, -0.22, 0.18)
    return jnp.clip(values, -most, most).astype(held_as)


def setup_inputs(seed: int = 0, part: int = 0) -> dict:
    key_of = jax.random.split(jax.random.key(seed), 11)
    part_splits = jax.random.split(jax.random.fold_in(key_of[10], part), 11)
    return {
        "layer_inputs": gaussian(part_splits[0], (LAYERS, NODES, D), 1.0, 6.0, ((0, 4), (1, 4)), jnp.float32),
        "pre_acts": gaussian(part_splits[1], (LAYERS, NODES, D), 1.0, 6.0, ((0, 4), (1, 4)), jnp.float32),
        "layer_outputs": gaussian(part_splits[2], (LAYERS, NODES, D), 1.0, 6.0, ((0, 4), (1, 4)), jnp.float32),
        "multipliers": gaussian(part_splits[3], (LAYERS, NODES, D), 1.0, 6.0, ((0, 4), (1, 4)), jnp.float32),
        "weights": gaussian(part_splits[4], (LAYERS, D, D), D ** -0.5, 0.25, ((0, 4),), jnp.float32),
        "biases": gaussian(part_splits[5], (LAYERS, D), 0.5, 3.0, ((0, 4),), jnp.float32),
        "prev_outputs": gaussian(part_splits[6], (NODES, D), 1.0, 6.0, ((0, 4),), jnp.float32),
        "prev_multipliers": gaussian(part_splits[7], (NODES, D), 1.0, 6.0, ((0, 4),), jnp.float32),
        "next_inputs": gaussian(part_splits[8], (NODES, D), 1.0, 6.0, ((0, 4),), jnp.float32),
        "row_order": jax.vmap(lambda own: jax.random.permutation(own, ROWS))(jax.random.split(part_splits[9], N_DP)).reshape((N_DP, ROWS)).astype(jnp.int32),
    }


penalty_nu = 1.0
penalty_rho = 1.0
step_input = 0.2
step_weight = 0.3
step_preact = 0.5


def matmul(form, left, right):
    return jnp.einsum(form, left, right, precision=lax.Precision.HIGHEST)


def reference(layer_inputs, pre_acts, layer_outputs, multipliers, weights, biases, prev_outputs, prev_multipliers, next_inputs, row_order):
    blocks = row_order.shape[0]
    base = (jnp.arange(blocks, dtype=jnp.int32) * ROWS)[:, None]
    gathered = (row_order.astype(jnp.int32) + base).reshape(-1)
    edge_outputs = jnp.take(prev_outputs, gathered, axis=0)
    edge_duals = jnp.take(prev_multipliers, gathered, axis=0)
    edge_inputs = jnp.take(next_inputs, gathered, axis=0)
    row_count = layer_inputs.shape[1]
    inputs, preact, outputs, duals = layer_inputs, pre_acts, layer_outputs, multipliers
    weight, offset = weights, biases
    for outer_pass in range(PASSES):
        before_out = jnp.concatenate([edge_outputs[None], outputs[:-1]], axis=0)
        before_dual = jnp.concatenate([edge_duals[None], duals[:-1]], axis=0)
        residual = matmul("lmd,lde->lme", inputs, weight) + offset[:, None, :] - preact
        back = matmul("lme,lde->lmd", residual, weight)
        inputs = inputs - step_input * (penalty_nu * back + before_dual + penalty_rho * (inputs - before_out))
        for inner_step in range(INNER):
            residual = matmul("lmd,lde->lme", inputs, weight) + offset[:, None, :] - preact
            grad_weight = matmul("lmd,lme->lde", inputs, residual)
            grad_offset = jnp.sum(residual, axis=1)
            weight = weight - (step_weight / row_count) * grad_weight
            offset = offset - (step_weight / row_count) * grad_offset
        target = matmul("lmd,lde->lme", inputs, weight) + offset[:, None, :]
        preact = preact - step_preact * ((preact - target) + (jax.nn.softplus(preact) - outputs) * jax.nn.sigmoid(preact))
        after_in = jnp.concatenate([inputs[1:], edge_inputs[None]], axis=0)
        outputs = (penalty_nu * jax.nn.softplus(preact) + duals + penalty_rho * after_in) / (penalty_nu + penalty_rho)
        duals = duals + penalty_rho * (after_in - outputs)
    return inputs, preact, outputs, duals, weight, offset
```

```python
import functools

import jax
import jax.numpy as jnp
from jax import lax
from jax.experimental import pallas as pl
from jax.experimental.pallas import tpu as pltpu
from jax.sharding import PartitionSpec as P

INNER = 3


penalty_nu = 1.0
penalty_rho = 1.0
step_input = 0.2
step_weight = 0.3
step_preact = 0.5


def from_behind(x, axis, by):
    count = lax.axis_size(axis)
    pairs = [(i, i + by) for i in range(count) if 0 <= i + by < count]
    return lax.ppermute(x, axis, pairs)


def matmul(left, right):
    return jnp.dot(left, right, precision=lax.Precision.HIGHEST)


def summed_body(
    layer_inputs,
    pre_acts,
    layer_outputs,
    multipliers,
    weights,
    biases,
    prev_outputs,
    prev_multipliers,
    next_inputs,
    row_order,
):
    row_perm = row_order[0]
    edge_outputs = jnp.take(prev_outputs, row_perm, axis=0)
    edge_duals = jnp.take(prev_multipliers, row_perm, axis=0)
    edge_inputs = jnp.take(next_inputs, row_perm, axis=0)
    first_layer = lax.axis_index("layer") == 0
    last_layer = lax.axis_index("layer") == lax.axis_size("layer") - 1
    row_count = layer_inputs.shape[1] * lax.axis_size("dp")
    scale = step_weight / row_count
    inputs, preact, outputs, duals = (
        layer_inputs[0],
        pre_acts[0],
        layer_outputs[0],
        multipliers[0],
    )
    weight, offset = (weights[0], biases[0])
    before_out, before_dual = from_behind((outputs, duals), "layer", 1)
    before_out = jnp.where(first_layer, edge_outputs, before_out)
    before_dual = jnp.where(first_layer, edge_duals, before_dual)
    coupling = before_dual + penalty_rho * (inputs - before_out)
    residual = matmul(inputs, weight) + offset[None, :] - preact
    inputs = inputs - step_input * (penalty_nu * matmul(residual, weight.T) + coupling)
    gram_matrix, cross_term, column_sums, preact_sums = lax.psum(
        (
            matmul(inputs.T, inputs),
            matmul(inputs.T, preact),
            jnp.sum(inputs, axis=0),
            jnp.sum(preact, axis=0),
        ),
        "dp",
    )
    for inner_step in range(INNER):
        grad_weight = (
            matmul(gram_matrix, weight) + column_sums[:, None] * offset[None, :] - cross_term
        )
        grad_offset = matmul(column_sums[None, :], weight)[0] + row_count * offset - preact_sums
        weight = weight - scale * grad_weight
        offset = offset - scale * grad_offset
    target = matmul(inputs, weight) + offset[None, :]
    preact = preact - step_preact * (
        preact - target + (jax.nn.softplus(preact) - outputs) * jax.nn.sigmoid(preact)
    )
    after_in = from_behind(inputs, "layer", -1)
    after_in = jnp.where(last_layer, edge_inputs, after_in)
    outputs = (penalty_nu * jax.nn.softplus(preact) + duals + penalty_rho * after_in) / (
        penalty_nu + penalty_rho
    )
    duals = duals + penalty_rho * (after_in - outputs)
    return (inputs[None], preact[None], outputs[None], duals[None], weight[None], offset[None])


MESH = pl.DeviceIdType.MESH
VMEM_BYTES = 67043328
NN = (((1,), (0,)), ((), ()))
NT = (((1,), (1,)), ((), ()))


def split(x):
    high = x.astype(jnp.bfloat16)
    return high, (x - high.astype(jnp.float32)).astype(jnp.bfloat16)


def dot3(left, right, dims=NN):
    def one(a, b):
        return lax.dot_general(a, b, dims, preferred_element_type=jnp.float32)

    return one(left[0], right[0]) + (one(left[0], right[1]) + one(left[1], right[0]))


def softplus(v):
    return jnp.maximum(v, 0.0) + jnp.log1p(jnp.exp(-jnp.abs(v)))


def permuted(order, x):
    rows = x.shape[0]
    stored = lax.broadcasted_iota(jnp.int32, (rows, rows), 0)
    pick = jnp.where(stored == order, 1.0, 0.0).T.astype(jnp.bfloat16)
    high, rest = split(x)
    rest = x - high.astype(jnp.float32)
    mid, low = split(rest)

    def one(part):
        return jnp.dot(pick, part, preferred_element_type=jnp.float32)

    return one(high) + (one(mid) + one(low))


def column_pieces(width):
    quarter = width // 4
    return [pl.ds(0 * quarter, 2 * quarter), pl.ds(2 * quarter, 2 * quarter)]


def kernel(
    n, layers,
    p_hbm, z_hbm, q_hbm, u_hbm, w_hbm, b_hbm, qb_hbm, ub_hbm, pb_hbm, order_hbm,
    p_out, z_out, q_out, u_out, w_out, b_out,
    p_ref, z_ref, q_ref, u_ref, w_ref, b_ref, qb_ref, ub_ref, pb_ref, order_ref,
    p_all, z_all, coupling, p_next, own_coupling, w_hi, w_lo, p_hi, p_lo, pt_hi, pt_lo, target0, t_hi, t_lo, change, z_part, q_part,
    z_right, z_left, z_recv, p_right, p_left, p_recv, layer_send, layer_recv, loads, ready,
):
    rows, width = p_ref.shape
    total = rows * n
    me, layer = lax.axis_index("dp"), lax.axis_index("layer")
    scale = step_weight / total
    has_left, has_right = me > 0, me < n - 1
    has_below, has_above = layer > 0, layer < layers - 1
    columns, halves = column_pieces(width), p_recv.shape[1]
    pieces = len(columns)
    row_half = [pl.ds(i * (rows // halves), rows // halves) for i in range(halves)]

    middle = n // 2
    tells_right, tells_left = jnp.logical_and(has_right, me < middle), me > middle
    told_by_left, told_by_right = jnp.logical_and(has_left, me <= middle), jnp.logical_and(has_right, me >= middle)

    barrier = pltpu.get_barrier_semaphore()
    for there, axis, index in (
        (tells_right, "dp", me + 1), (tells_left, "dp", me - 1),
        (has_below, "layer", layer - 1), (has_above, "layer", layer + 1),
    ):
        @pl.when(there)
        def _():
            pl.semaphore_signal(barrier, inc=1, device_id={axis: index}, device_id_type=MESH)

    load = {}
    for i, (name, source, target) in enumerate((
        ("u", u_hbm, u_ref), ("q", q_hbm, q_ref), ("w", w_hbm, w_ref), ("p", p_hbm, p_ref), ("b", b_hbm, b_ref),
        ("z", z_hbm, z_ref), ("order", order_hbm, order_ref), ("ub", ub_hbm, ub_ref), ("qb", qb_hbm, qb_ref),
        ("pb", pb_hbm, pb_ref),
    )):
        load[name] = pltpu.make_async_copy(source, target, loads.at[i])
        load[name].start()

    def z_copy(owner, i, to_right, own=False):
        return pltpu.make_async_remote_copy(
            src_ref=(z_hbm if own else z_all.at[owner]).at[:, columns[i]], dst_ref=z_all.at[owner, :, columns[i]],
            send_sem=(z_right if to_right else z_left).at[owner, i], recv_sem=z_recv.at[owner, i],
            device_id={"dp": me + 1 if to_right else me - 1}, device_id_type=MESH,
        )

    def p_copy(owner, i, to_right):
        return pltpu.make_async_remote_copy(
            src_ref=p_all.at[owner, row_half[i]], dst_ref=p_all.at[owner, row_half[i]],
            send_sem=(p_right if to_right else p_left).at[owner, i], recv_sem=p_recv.at[owner, i],
            device_id={"dp": me + 1 if to_right else me - 1}, device_id_type=MESH,
        )

    up = pltpu.make_async_remote_copy(
        src_ref=own_coupling, dst_ref=coupling, send_sem=layer_send.at[0], recv_sem=layer_recv.at[0],
        device_id={"layer": layer + 1}, device_id_type=MESH,
    )
    down = pltpu.make_async_remote_copy(
        src_ref=p_all.at[me], dst_ref=p_next, send_sem=layer_send.at[1], recv_sem=layer_recv.at[1],
        device_id={"layer": layer - 1}, device_id_type=MESH,
    )

    def send(copy, indices, to_right):
        @pl.when(has_right if to_right else has_left)
        def _():
            for i in indices:
                copy(me, i, to_right).start()

    near_left = me < n // 2

    def relay(s, copy, indices):
        def leftward():
            for i in indices:
                copy(me + s, i, False).wait_recv()
                copy(me + s, i, False).start()

        to_left = jnp.logical_and(me + s < n, has_left)
        pl.when(jnp.logical_and(to_left, near_left))(leftward)

        @pl.when(jnp.logical_and(me >= s, has_right))
        def _():
            for i in indices:
                copy(me - s, i, True).wait_recv()
                copy(me - s, i, True).start()

        pl.when(jnp.logical_and(to_left, jnp.logical_not(near_left)))(leftward)

    def arrive(s, copy, indices):
        @pl.when(jnp.logical_and(me >= s, jnp.logical_not(has_right)))
        def _():
            for i in indices:
                copy(me - s, i, True).wait_recv()

        @pl.when(jnp.logical_and(me + s < n, jnp.logical_not(has_left)))
        def _():
            for i in indices:
                copy(me + s, i, False).wait_recv()

    def use(s, step):
        pl.when(me >= s)(lambda: step(me - s))
        pl.when(me + s < n)(lambda: step(me + s))

    ends = [jnp.where(there, 1, 0) for there in (told_by_left, told_by_right, has_below, has_above)]
    pl.semaphore_wait(barrier, ends[0] + ends[1] + ends[2] + ends[3])
    own_z = functools.partial(z_copy, own=True)

    @pl.when(told_by_left)
    def _():
        for i in range(pieces):
            own_z(me, i, False).start()
        pl.semaphore_signal(ready.at[0], inc=1, device_id={"dp": me - 1}, device_id_type=MESH)

    @pl.when(told_by_right)
    def _():
        for i in range(pieces):
            own_z(me, i, True).start()
        pl.semaphore_signal(ready.at[1], inc=1, device_id={"dp": me + 1}, device_id_type=MESH)

    load["u"].wait()
    load["q"].wait()
    own_coupling[...] = u_ref[...] - q_ref[...]
    pl.when(has_above)(lambda: up.start())

    for name in ("w", "p", "b", "z", "order", "ub", "qb", "pb"):
        load[name].wait()
    w_hi[...], w_lo[...] = split(w_ref[...])
    weight = (w_hi[...], w_lo[...])
    p, z, bias = p_ref[...], z_ref[...], b_ref[...]
    residual = dot3(split(p), weight) + bias - z

    @pl.when(tells_right)
    def _():
        pl.semaphore_wait(ready.at[0], 1)
        for i in range(pieces):
            own_z(me, i, True).start()

    @pl.when(tells_left)
    def _():
        pl.semaphore_wait(ready.at[1], 1)
        for i in range(pieces):
            own_z(me, i, False).start()

    back = dot3(split(residual), weight, NT)

    @pl.when(jnp.logical_not(has_below))
    def _():
        coupling[...] = permuted(order_ref[...], ub_ref[...] - qb_ref[...])

    pl.when(has_below)(lambda: up.wait_recv())
    p = p - step_input * (back + (coupling[...] + p))
    p_all[me] = p
    send(p_copy, range(halves), False)
    send(p_copy, range(halves), True)
    pl.when(has_below)(lambda: down.start())
    first, rest = range(1), range(1, pieces)
    relay(1, z_copy, first)
    p_out[...] = p

    @pl.when(jnp.logical_not(has_above))
    def _():
        p_next[...] = permuted(order_ref[...], pb_ref[...])

    pt_hi[pl.ds(width, 16), :] = jnp.ones((16, total), jnp.bfloat16)
    pt_lo[pl.ds(width, 16), :] = jnp.zeros((16, total), jnp.bfloat16)

    def block(owner):
        return pl.ds(pl.multiple_of(owner * rows, rows), rows)

    def take_p(owner):
        value = p_all[owner]
        high, low = split(value)
        p_hi[block(owner), :], p_lo[block(owner), :] = high, low
        across = split(value.T)
        pt_hi[pl.ds(0, width), block(owner)] = across[0]
        pt_lo[pl.ds(0, width), block(owner)] = across[1]
        target0[block(owner), :] = dot3((high, low), (w_hi[...], w_lo[...])) + b_ref[...]

    def take_above():
        pl.when(has_above)(lambda: down.wait_recv())
        q_part[...] = penalty_rho * p_next[...] + u_ref[...]

    take_p(me)
    z, q = z_ref[...], q_ref[...]
    target0[block(me), :] -= z
    z_part[...] = z - step_preact * (z + (softplus(z) - q) * jax.nn.sigmoid(z))
    for s in range(1, n):
        relay(s, p_copy, range(halves))
        if s > 1 and s < n - 1:
            relay(s - 1, z_copy, rest)
            relay(s, z_copy, first)
        arrive(s, p_copy, range(halves))
        use(s, take_p)
        if s == 1:
            take_above()
    if n == 1:
        take_above()
    if n > 2:
        relay(n - 2, z_copy, rest)

    stacked = (p_hi[...], p_lo[...])
    moment = scale * (dot3(stacked, stacked, NT) + 1.0)
    moment_parts = split(moment)
    same = lax.broadcasted_iota(jnp.int32, (total, total), 0) == lax.broadcasted_iota(jnp.int32, (total, total), 1)
    steps = jnp.where(same, 3.0, 0.0) - 3.0 * moment + dot3(moment_parts, moment_parts)
    t = scale * dot3((pt_hi[...], pt_lo[...]), split(steps))
    t_hi[...], t_lo[...] = split(t)

    def take_z(owner):
        target0[block(owner), :] -= z_all[owner]

    for s in range(1, n - 1):
        arrive(s, z_copy, range(pieces))
        use(s, take_z)
    change[...] = dot3((t_hi[...], t_lo[...]), split(target0[...]))
    for owner in range(n):
        @pl.when(jnp.logical_and(me >= owner, has_right))
        def _():
            for i in range(halves):
                p_copy(owner, i, True).wait_send()
        @pl.when(jnp.logical_and(me <= owner, has_left))
        def _():
            for i in range(halves):
                p_copy(owner, i, False).wait_send()
    pl.when(has_above)(lambda: up.wait_send())
    pl.when(has_below)(lambda: down.wait_send())
    p_parts = split(p_all[me])
    z_out[:, columns[-1]] = z_part[:, columns[-1]]
    q_out[:, columns[-1]] = q_part[:, columns[-1]]
    for i, some in enumerate(columns):
        def add(owner):
            change[:, some] -= dot3((t_hi[:, block(owner)], t_lo[:, block(owner)]), split(z_all[owner, :, some]))

        if n > 1:
            arrive(n - 1, z_copy, [i])
            use(n - 1, add)
        w = w_ref[:, some] - change[pl.ds(0, width), some]
        bias = b_ref[:, some] - change[pl.ds(width, 1), some]
        w_out[:, some] = w
        b_out[:, some] = bias
        if i == pieces - 1:
            break
        z = z_part[:, some] + step_preact * (dot3(p_parts, split(w)) + bias)
        z_out[:, some] = z
        known = q_part[:, some]
        q = (penalty_nu * softplus(z) + known) / (penalty_nu + penalty_rho)
        q_out[:, some] = q
        u_out[:, some] = known - penalty_rho * q

    for owner in range(n):
        @pl.when(jnp.logical_and(me >= owner, has_right))
        def _():
            for i in range(pieces):
                z_copy(owner, i, True).wait_send()
        @pl.when(jnp.logical_and(me <= owner, has_left))
        def _():
            for i in range(pieces):
                z_copy(owner, i, False).wait_send()


def last_kernel(
    p_ref, z_ref, q_ref, u_ref, w_ref, b_ref, p_hbm, z_hbm, q_hbm, u_hbm, w_hbm, b_hbm, z_last, q_last, u_last, sems
):
    width = p_ref.shape[1]
    last = column_pieces(width)[-1]
    done = pl.ds(0, last.start)
    copies = [pltpu.make_async_copy(a, b, sems.at[i]) for i, (a, b) in enumerate((
        (w_ref, w_hbm), (p_ref, p_hbm), (b_ref, b_hbm), (z_ref.at[:, done], z_hbm.at[:, done]),
        (q_ref.at[:, done], q_hbm.at[:, done]), (u_ref.at[:, done], u_hbm.at[:, done]),
        (z_last, z_hbm.at[:, last]), (q_last, q_hbm.at[:, last]), (u_last, u_hbm.at[:, last]),
    ))]
    for copy in copies[:6]:
        copy.start()
    z = z_ref[:, last] + step_preact * (dot3(split(p_ref[...]), split(w_ref[:, last])) + b_ref[:, last])
    z_last[...] = z
    copies[6].start()
    known = q_ref[:, last]
    q = (penalty_nu * softplus(z) + known) / (penalty_nu + penalty_rho)
    q_last[...] = q
    copies[7].start()
    u_last[...] = known - penalty_rho * q
    copies[8].start()
    for copy in copies:
        copy.wait()


def gathered_body(n, layers, layer_inputs, pre_acts, layer_outputs, multipliers, weights, biases, prev_outputs, prev_multipliers, next_inputs, row_order):
    rows, width = prev_outputs.shape
    total = rows * n
    pieces, halves = len(column_pieces(width)), 2
    f32, b16 = jnp.float32, jnp.bfloat16
    dma = pltpu.SemaphoreType.DMA
    block = jax.ShapeDtypeStruct((rows, width), f32)
    hbm = pl.BlockSpec(memory_space=pltpu.HBM)
    shapes = (block,) * 4 + (jax.ShapeDtypeStruct((width, width), f32), jax.ShapeDtypeStruct((1, width), f32))
    vm = pl.BlockSpec(memory_space=pltpu.VMEM)
    kept = (sum(x.size for x in shapes) * 4 + 2**14) // 2**12 * 2**12
    outs = pl.pallas_call(
        functools.partial(kernel, n, layers),
        out_shape=tuple(pltpu.VMEM(x.shape, x.dtype) for x in shapes),
        in_specs=[hbm] * 10,
        out_specs=(vm,) * 6,
        scratch_shapes=[
            *(pltpu.VMEM((rows, width), f32),) * 4,
            pltpu.VMEM((width, width), f32), pltpu.VMEM((1, width), f32),
            *(pltpu.VMEM((rows, width), f32),) * 3,
            pltpu.VMEM((1, rows), jnp.int32),
            pltpu.VMEM((n, rows, width), f32), pltpu.VMEM((n, rows, width), f32),
            pltpu.VMEM((rows, width), f32), pltpu.VMEM((rows, width), f32), pltpu.VMEM((rows, width), f32),
            pltpu.VMEM((width, width), b16), pltpu.VMEM((width, width), b16),
            pltpu.VMEM((total, width), b16), pltpu.VMEM((total, width), b16),
            pltpu.VMEM((width + 16, total), b16), pltpu.VMEM((width + 16, total), b16),
            pltpu.VMEM((total, width), f32),
            pltpu.VMEM((width + 16, total), b16), pltpu.VMEM((width + 16, total), b16),
            pltpu.VMEM((width + 16, width), f32), pltpu.VMEM((rows, width), f32), pltpu.VMEM((rows, width), f32),
            *(dma((n, pieces)),) * 3, *(dma((n, halves)),) * 3, dma((2,)), dma((2,)), dma((10,)), pltpu.SemaphoreType.REGULAR((2,)),
        ],
        compiler_params=pltpu.CompilerParams(collective_id=0, has_side_effects=True, vmem_limit_bytes=VMEM_BYTES - kept),
    )(layer_inputs[0], pre_acts[0], layer_outputs[0], multipliers[0], weights[0], biases, prev_outputs, prev_multipliers, next_inputs, row_order)
    outs = pl.pallas_call(
        last_kernel, out_shape=shapes, in_specs=[vm] * 6, out_specs=(hbm,) * 6,
        scratch_shapes=[*(pltpu.VMEM((rows, column_pieces(width)[-1].size), f32),) * 3, dma((9,))],
        compiler_params=pltpu.CompilerParams(vmem_limit_bytes=2**22),
    )(*outs)
    return tuple(x[None] for x in outs[:5]) + (outs[5],)


def solution(mesh):
    n, layers = mesh.shape["dp"], mesh.shape["layer"]
    body = functools.partial(gathered_body, n, layers) if n <= 8 else summed_body
    return jax.shard_map(
        body,
        mesh=mesh,
        in_specs=(
            P("layer", ("groups", "dp"), None),
            P("layer", ("groups", "dp"), None),
            P("layer", ("groups", "dp"), None),
            P("layer", ("groups", "dp"), None),
            P(("groups", "layer"), None, None),
            P(("groups", "layer"), None),
            P(("groups", "dp"), None),
            P(("groups", "dp"), None),
            P(("groups", "dp"), None),
            P(("groups", "dp"), None),
        ),
        out_specs=(
            P("layer", ("groups", "dp"), None),
            P("layer", ("groups", "dp"), None),
            P("layer", ("groups", "dp"), None),
            P("layer", ("groups", "dp"), None),
            P(("groups", "layer"), None, None),
            P(("groups", "layer"), None),
        ),
        check_vma=False,
    )
```

```python
import functools

import jax
import jax.numpy as jnp
from jax import lax
from jax.experimental import pallas as pl
from jax.experimental.pallas import tpu as pltpu
from jax.sharding import PartitionSpec as P

INNER = 3


penalty_nu = 1.0
penalty_rho = 1.0
step_input = 0.2
step_weight = 0.3
step_preact = 0.5


def from_behind(x, axis, by):
    count = lax.axis_size(axis)
    pairs = [(i, i + by) for i in range(count) if 0 <= i + by < count]
    return lax.ppermute(x, axis, pairs)


def matmul(left, right):
    return jnp.dot(left, right, precision=lax.Precision.HIGHEST)


def summed_body(
    layer_inputs,
    pre_acts,
    layer_outputs,
    multipliers,
    weights,
    biases,
    prev_outputs,
    prev_multipliers,
    next_inputs,
    row_order,
):
    row_perm = row_order[0]
    edge_outputs = jnp.take(prev_outputs, row_perm, axis=0)
    edge_duals = jnp.take(prev_multipliers, row_perm, axis=0)
    edge_inputs = jnp.take(next_inputs, row_perm, axis=0)
    first_layer = lax.axis_index("layer") == 0
    last_layer = lax.axis_index("layer") == lax.axis_size("layer") - 1
    row_count = layer_inputs.shape[1] * lax.axis_size("dp")
    scale = step_weight / row_count
    inputs, preact, outputs, duals = (
        layer_inputs[0],
        pre_acts[0],
        layer_outputs[0],
        multipliers[0],
    )
    weight, offset = (weights[0], biases[0])
    before_out, before_dual = from_behind((outputs, duals), "layer", 1)
    before_out = jnp.where(first_layer, edge_outputs, before_out)
    before_dual = jnp.where(first_layer, edge_duals, before_dual)
    coupling = before_dual + penalty_rho * (inputs - before_out)
    residual = matmul(inputs, weight) + offset[None, :] - preact
    inputs = inputs - step_input * (penalty_nu * matmul(residual, weight.T) + coupling)
    gram_matrix, cross_term, column_sums, preact_sums = lax.psum(
        (
            matmul(inputs.T, inputs),
            matmul(inputs.T, preact),
            jnp.sum(inputs, axis=0),
            jnp.sum(preact, axis=0),
        ),
        "dp",
    )
    for inner_step in range(INNER):
        grad_weight = (
            matmul(gram_matrix, weight) + column_sums[:, None] * offset[None, :] - cross_term
        )
        grad_offset = matmul(column_sums[None, :], weight)[0] + row_count * offset - preact_sums
        weight = weight - scale * grad_weight
        offset = offset - scale * grad_offset
    target = matmul(inputs, weight) + offset[None, :]
    preact = preact - step_preact * (
        preact - target + (jax.nn.softplus(preact) - outputs) * jax.nn.sigmoid(preact)
    )
    after_in = from_behind(inputs, "layer", -1)
    after_in = jnp.where(last_layer, edge_inputs, after_in)
    outputs = (penalty_nu * jax.nn.softplus(preact) + duals + penalty_rho * after_in) / (
        penalty_nu + penalty_rho
    )
    duals = duals + penalty_rho * (after_in - outputs)
    return (inputs[None], preact[None], outputs[None], duals[None], weight[None], offset[None])


MESH = pl.DeviceIdType.MESH
VMEM_BYTES = 67043328
NN = (((1,), (0,)), ((), ()))
NT = (((1,), (1,)), ((), ()))


def split(x):
    high = x.astype(jnp.bfloat16)
    return high, (x - high.astype(jnp.float32)).astype(jnp.bfloat16)


def dot3(left, right, dims=NN):
    def one(a, b):
        return lax.dot_general(a, b, dims, preferred_element_type=jnp.float32)

    return one(left[0], right[0]) + (one(left[0], right[1]) + one(left[1], right[0]))


def softplus(v):
    return jnp.maximum(v, 0.0) + jnp.log1p(jnp.exp(-jnp.abs(v)))


def permuted(order, x):
    rows = x.shape[0]
    stored = lax.broadcasted_iota(jnp.int32, (rows, rows), 0)
    pick = jnp.where(stored == order, 1.0, 0.0).T.astype(jnp.bfloat16)
    high, rest = split(x)
    rest = x - high.astype(jnp.float32)
    mid, low = split(rest)

    def one(part):
        return jnp.dot(pick, part, preferred_element_type=jnp.float32)

    return one(high) + (one(mid) + one(low))


def column_halves(width):
    return [pl.ds(0, width // 2), pl.ds(width // 2, width // 2)]


def z_pieces(rows, width):
    left, right = column_halves(width)
    some = pl.ds(0, 96 * rows // 128)
    return [(pl.ds(0, rows), left), (pl.ds(some.size, rows - some.size), right), (some, right)]


def kernel(
    n, layers,
    p_hbm, z_hbm, q_hbm, u_hbm, w_hbm, b_hbm, qb_hbm, ub_hbm, pb_hbm, order_hbm,
    p_out, z_out, q_out, u_out, w_out, b_out,
    p_ref, z_ref, q_ref, u_ref, w_ref, b_ref, qb_ref, ub_ref, pb_ref, order_ref,
    p_all, z_all, aside, coupling, p_next, own_coupling, w_hi, w_lo, p_hi, p_lo, pt_hi, pt_lo, target0, t_hi, t_lo, change, z_part, q_part,
    z_right, z_left, z_recv, p_right, p_left, p_recv, layer_send, layer_recv, loads, ready, aside_send, aside_recv,
):
    rows, width = p_ref.shape
    total = rows * n
    me, layer = lax.axis_index("dp"), lax.axis_index("layer")
    scale = step_weight / total
    has_left, has_right = me > 0, me < n - 1
    has_below, has_above = layer > 0, layer < layers - 1
    columns, parts, halves = column_halves(width), z_pieces(rows, width), p_recv.shape[1]
    pieces = len(parts)
    row_half = [pl.ds(i * (rows // halves), rows // halves) for i in range(halves)]

    middle = n // 2
    tells_right, tells_left = jnp.logical_and(has_right, me < middle), me > middle
    told_by_left, told_by_right = jnp.logical_and(has_left, me <= middle), jnp.logical_and(has_right, me >= middle)

    barrier = pltpu.get_barrier_semaphore()
    for there, axis, index in (
        (tells_right, "dp", me + 1), (tells_left, "dp", me - 1),
        (has_below, "layer", layer - 1), (has_above, "layer", layer + 1),
    ):
        @pl.when(there)
        def _():
            pl.semaphore_signal(barrier, inc=1, device_id={axis: index}, device_id_type=MESH)

    load = {}
    for i, (name, source, target) in enumerate((
        ("u", u_hbm, u_ref), ("q", q_hbm, q_ref), ("w", w_hbm, w_ref), ("p", p_hbm, p_ref), ("b", b_hbm, b_ref),
        ("z", z_hbm, z_ref), ("order", order_hbm, order_ref), ("ub", ub_hbm, ub_ref), ("qb", qb_hbm, qb_ref),
        ("pb", pb_hbm, pb_ref),
    )):
        load[name] = pltpu.make_async_copy(source, target, loads.at[i])
        load[name].start()

    def z_copy(owner, i, to_right, own=False):
        return pltpu.make_async_remote_copy(
            src_ref=(z_hbm if own else z_all.at[owner]).at[*parts[i]], dst_ref=z_all.at[owner, *parts[i]],
            send_sem=(z_right if to_right else z_left).at[owner, i], recv_sem=z_recv.at[owner, i],
            device_id={"dp": me + 1 if to_right else me - 1}, device_id_type=MESH,
        )

    def p_copy(owner, i, to_right):
        return pltpu.make_async_remote_copy(
            src_ref=p_all.at[owner, row_half[i]], dst_ref=p_all.at[owner, row_half[i]],
            send_sem=(p_right if to_right else p_left).at[owner, i], recv_sem=p_recv.at[owner, i],
            device_id={"dp": me + 1 if to_right else me - 1}, device_id_type=MESH,
        )

    up = pltpu.make_async_remote_copy(
        src_ref=own_coupling, dst_ref=coupling, send_sem=layer_send.at[0], recv_sem=layer_recv.at[0],
        device_id={"layer": layer + 1}, device_id_type=MESH,
    )
    down = pltpu.make_async_remote_copy(
        src_ref=p_all.at[me], dst_ref=p_next, send_sem=layer_send.at[1], recv_sem=layer_recv.at[1],
        device_id={"layer": layer - 1}, device_id_type=MESH,
    )

    def send(copy, indices, to_right):
        @pl.when(has_right if to_right else has_left)
        def _():
            for i in indices:
                copy(me, i, to_right).start()

    near_left = me < n // 2

    def relay(s, copy, indices):
        def leftward():
            for i in indices:
                if copy is z_copy and has_aside and s == 1 and i == turned:
                    @pl.when(jnp.logical_not(leaves))
                    def _():
                        copy(me + s, i, False).wait_recv()
                        copy(me + s, i, False).start()
                else:
                    copy(me + s, i, False).wait_recv()
                    copy(me + s, i, False).start()

        to_left = jnp.logical_and(me + s < n, has_left)
        pl.when(jnp.logical_and(to_left, near_left))(leftward)

        @pl.when(jnp.logical_and(me >= s, has_right))
        def _():
            for i in indices:
                copy(me - s, i, True).wait_recv()
                copy(me - s, i, True).start()

        pl.when(jnp.logical_and(to_left, jnp.logical_not(near_left)))(leftward)

    turned, way = pieces - 1, min(2, n - 1)
    has_aside = n > 2 and layers > 2
    leaves = jnp.logical_and(layer == 0, me == 1)
    passes = jnp.logical_and(layer == 2, me == 1)
    returns = jnp.logical_and(layer == 2, me == 0)
    asides = [
        pltpu.make_async_remote_copy(
            src_ref=source, dst_ref=target, send_sem=aside_send.at[0], recv_sem=received,
            device_id=there, device_id_type=MESH,
        )
        for source, target, received, there in (
            (z_all.at[way, *parts[turned]], aside, aside_recv.at[0], {"layer": layer + 2}),
            (aside, aside, aside_recv.at[1], {"dp": me - 1}),
            (aside, z_all.at[way, *parts[turned]], z_recv.at[way, turned], {"layer": layer - 2}),
        )
    ]

    def arrive(s, copy, indices):
        @pl.when(jnp.logical_and(me >= s, jnp.logical_not(has_right)))
        def _():
            for i in indices:
                copy(me - s, i, True).wait_recv()

        @pl.when(jnp.logical_and(me + s < n, jnp.logical_not(has_left)))
        def _():
            for i in indices:
                copy(me + s, i, False).wait_recv()

    def use(s, step):
        pl.when(me >= s)(lambda: step(me - s))
        pl.when(me + s < n)(lambda: step(me + s))

    ends = [jnp.where(there, 1, 0) for there in (told_by_left, told_by_right, has_below, has_above)]
    pl.semaphore_wait(barrier, ends[0] + ends[1] + ends[2] + ends[3])
    own_z = functools.partial(z_copy, own=True)

    @pl.when(told_by_left)
    def _():
        for i in range(pieces):
            own_z(me, i, False).start()
        pl.semaphore_signal(ready.at[0], inc=1, device_id={"dp": me - 1}, device_id_type=MESH)

    @pl.when(told_by_right)
    def _():
        for i in range(pieces):
            own_z(me, i, True).start()
        pl.semaphore_signal(ready.at[1], inc=1, device_id={"dp": me + 1}, device_id_type=MESH)

    load["u"].wait()
    load["q"].wait()
    own_coupling[...] = u_ref[...] - q_ref[...]
    pl.when(has_above)(lambda: up.start())

    for name in ("w", "p", "b", "z", "order", "ub", "qb", "pb"):
        load[name].wait()
    w_hi[...], w_lo[...] = split(w_ref[...])
    weight = (w_hi[...], w_lo[...])
    p, z, bias = p_ref[...], z_ref[...], b_ref[...]
    residual = dot3(split(p), weight) + bias - z

    @pl.when(tells_right)
    def _():
        pl.semaphore_wait(ready.at[0], 1)
        for i in range(pieces):
            own_z(me, i, True).start()

    @pl.when(tells_left)
    def _():
        pl.semaphore_wait(ready.at[1], 1)
        for i in range(pieces):
            own_z(me, i, False).start()

    back = dot3(split(residual), weight, NT)

    @pl.when(jnp.logical_not(has_below))
    def _():
        coupling[...] = permuted(order_ref[...], ub_ref[...] - qb_ref[...])

    pl.when(has_below)(lambda: up.wait_recv())
    p = p - step_input * (back + (coupling[...] + p))
    p_all[me] = p
    send(p_copy, range(halves), False)
    send(p_copy, range(halves), True)
    pl.when(has_below)(lambda: down.start())
    first, rest = range(1), range(1, pieces)
    relay(1, z_copy, first)
    p_out[...] = p

    @pl.when(jnp.logical_not(has_above))
    def _():
        p_next[...] = permuted(order_ref[...], pb_ref[...])

    pt_hi[pl.ds(width, 16), :] = jnp.ones((16, total), jnp.bfloat16)
    pt_lo[pl.ds(width, 16), :] = jnp.zeros((16, total), jnp.bfloat16)

    def block(owner):
        return pl.ds(pl.multiple_of(owner * rows, rows), rows)

    def take_p(owner):
        value = p_all[owner]
        high, low = split(value)
        p_hi[block(owner), :], p_lo[block(owner), :] = high, low
        across = split(value.T)
        pt_hi[pl.ds(0, width), block(owner)] = across[0]
        pt_lo[pl.ds(0, width), block(owner)] = across[1]
        target0[block(owner), :] = dot3((high, low), (w_hi[...], w_lo[...])) + b_ref[...]

    def take_above():
        pl.when(has_above)(lambda: down.wait_recv())
        q_part[...] = penalty_rho * p_next[...] + u_ref[...]

    take_p(me)
    z, q = z_ref[...], q_ref[...]
    target0[block(me), :] -= z
    z_part[...] = z - step_preact * (z + (softplus(z) - q) * jax.nn.sigmoid(z))
    take_above()
    if has_aside:
        @pl.when(leaves)
        def _():
            z_copy(way, turned, False).wait_recv()
            asides[0].start()

        @pl.when(passes)
        def _():
            asides[0].wait_recv()
            asides[1].start()

    for s in range(1, n):
        relay(s, p_copy, range(halves))
        if s > 1 and s < n - 1:
            relay(s - 1, z_copy, rest)
            relay(s, z_copy, first)
        arrive(s, p_copy, range(halves))
        use(s, take_p)
        if s == 1 and has_aside:
            @pl.when(returns)
            def _():
                asides[1].wait_recv()
                asides[2].start()
    if n > 2:
        relay(n - 2, z_copy, rest)

    stacked = (p_hi[...], p_lo[...])
    moment = scale * (dot3(stacked, stacked, NT) + 1.0)
    moment_parts = split(moment)
    same = lax.broadcasted_iota(jnp.int32, (total, total), 0) == lax.broadcasted_iota(jnp.int32, (total, total), 1)
    steps = jnp.where(same, 3.0, 0.0) - 3.0 * moment + dot3(moment_parts, moment_parts)
    t = scale * dot3((pt_hi[...], pt_lo[...]), split(steps))
    t_hi[...], t_lo[...] = split(t)

    def take_z(owner):
        target0[block(owner), :] -= z_all[owner]

    for s in range(1, n - 1):
        arrive(s, z_copy, range(pieces))
        use(s, take_z)
    change[...] = dot3((t_hi[...], t_lo[...]), split(target0[...]))
    if has_aside:
        for there, copy in zip((leaves, passes, returns), asides):
            pl.when(there)(lambda: copy.wait_send())
    for owner in range(n):
        @pl.when(jnp.logical_and(me >= owner, has_right))
        def _():
            for i in range(halves):
                p_copy(owner, i, True).wait_send()
        @pl.when(jnp.logical_and(me <= owner, has_left))
        def _():
            for i in range(halves):
                p_copy(owner, i, False).wait_send()
    pl.when(has_above)(lambda: up.wait_send())
    pl.when(has_below)(lambda: down.wait_send())
    p_parts = split(p_all[me])
    z_out[:, columns[-1]] = z_part[:, columns[-1]]
    q_out[:, columns[-1]] = q_part[:, columns[-1]]
    for i, some in enumerate(columns):
        def add(owner):
            change[:, some] -= dot3((t_hi[:, block(owner)], t_lo[:, block(owner)]), split(z_all[owner, :, some]))

        if n > 1:
            arrive(n - 1, z_copy, [[0], [1, 2]][i])
            use(n - 1, add)
        w = w_ref[:, some] - change[pl.ds(0, width), some]
        bias = b_ref[:, some] - change[pl.ds(width, 1), some]
        w_out[:, some] = w
        b_out[:, some] = bias
        if i == len(columns) - 1:
            break
        z = z_part[:, some] + step_preact * (dot3(p_parts, split(w)) + bias)
        z_out[:, some] = z
        known = q_part[:, some]
        q = (penalty_nu * softplus(z) + known) / (penalty_nu + penalty_rho)
        q_out[:, some] = q
        u_out[:, some] = known - penalty_rho * q

    for owner in range(n):
        @pl.when(jnp.logical_and(me >= owner, has_right))
        def _():
            for i in range(pieces):
                z_copy(owner, i, True).wait_send()
        @pl.when(jnp.logical_and(me <= owner, has_left))
        def _():
            for i in range(pieces):
                if has_aside and owner == way and i == turned:
                    pl.when(jnp.logical_not(leaves))(lambda: z_copy(owner, i, False).wait_send())
                else:
                    z_copy(owner, i, False).wait_send()


def last_kernel(
    p_ref, z_ref, q_ref, u_ref, w_ref, b_ref, p_hbm, z_hbm, q_hbm, u_hbm, w_hbm, b_hbm, z_last, q_last, u_last, sems
):
    width = p_ref.shape[1]
    last = column_halves(width)[-1]
    done = pl.ds(0, last.start)
    copies = [pltpu.make_async_copy(a, b, sems.at[i]) for i, (a, b) in enumerate((
        (w_ref, w_hbm), (p_ref, p_hbm), (b_ref, b_hbm), (z_ref.at[:, done], z_hbm.at[:, done]),
        (q_ref.at[:, done], q_hbm.at[:, done]), (u_ref.at[:, done], u_hbm.at[:, done]),
        (z_last, z_hbm.at[:, last]), (q_last, q_hbm.at[:, last]), (u_last, u_hbm.at[:, last]),
    ))]
    for copy in copies[:6]:
        copy.start()
    z = z_ref[:, last] + step_preact * (dot3(split(p_ref[...]), split(w_ref[:, last])) + b_ref[:, last])
    z_last[...] = z
    copies[6].start()
    known = q_ref[:, last]
    q = (penalty_nu * softplus(z) + known) / (penalty_nu + penalty_rho)
    q_last[...] = q
    copies[7].start()
    u_last[...] = known - penalty_rho * q
    copies[8].start()
    for copy in copies:
        copy.wait()


def gathered_body(n, layers, layer_inputs, pre_acts, layer_outputs, multipliers, weights, biases, prev_outputs, prev_multipliers, next_inputs, row_order):
    rows, width = prev_outputs.shape
    total = rows * n
    parts, halves = z_pieces(rows, width), 2
    pieces = len(parts)
    f32, b16 = jnp.float32, jnp.bfloat16
    dma = pltpu.SemaphoreType.DMA
    block = jax.ShapeDtypeStruct((rows, width), f32)
    hbm = pl.BlockSpec(memory_space=pltpu.HBM)
    shapes = (block,) * 4 + (jax.ShapeDtypeStruct((width, width), f32), jax.ShapeDtypeStruct((1, width), f32))
    vm = pl.BlockSpec(memory_space=pltpu.VMEM)
    kept = (sum(x.size for x in shapes) * 4 + 2**14) // 2**12 * 2**12
    outs = pl.pallas_call(
        functools.partial(kernel, n, layers),
        out_shape=tuple(pltpu.VMEM(x.shape, x.dtype) for x in shapes),
        in_specs=[hbm] * 10,
        out_specs=(vm,) * 6,
        scratch_shapes=[
            *(pltpu.VMEM((rows, width), f32),) * 4,
            pltpu.VMEM((width, width), f32), pltpu.VMEM((1, width), f32),
            *(pltpu.VMEM((rows, width), f32),) * 3,
            pltpu.VMEM((1, rows), jnp.int32),
            pltpu.VMEM((n, rows, width), f32), pltpu.VMEM((n, rows, width), f32), pltpu.VMEM((parts[-1][0].size, parts[-1][1].size), f32),
            pltpu.VMEM((rows, width), f32), pltpu.VMEM((rows, width), f32), pltpu.VMEM((rows, width), f32),
            pltpu.VMEM((width, width), b16), pltpu.VMEM((width, width), b16),
            pltpu.VMEM((total, width), b16), pltpu.VMEM((total, width), b16),
            pltpu.VMEM((width + 16, total), b16), pltpu.VMEM((width + 16, total), b16),
            pltpu.VMEM((total, width), f32),
            pltpu.VMEM((width + 16, total), b16), pltpu.VMEM((width + 16, total), b16),
            pltpu.VMEM((width + 16, width), f32), pltpu.VMEM((rows, width), f32), pltpu.VMEM((rows, width), f32),
            *(dma((n, pieces)),) * 3, *(dma((n, halves)),) * 3, dma((2,)), dma((2,)), dma((10,)), pltpu.SemaphoreType.REGULAR((2,)),
            dma((1,)), dma((2,)),
        ],
        compiler_params=pltpu.CompilerParams(collective_id=0, has_side_effects=True, vmem_limit_bytes=VMEM_BYTES - kept),
    )(layer_inputs[0], pre_acts[0], layer_outputs[0], multipliers[0], weights[0], biases, prev_outputs, prev_multipliers, next_inputs, row_order)
    outs = pl.pallas_call(
        last_kernel, out_shape=shapes, in_specs=[vm] * 6, out_specs=(hbm,) * 6,
        scratch_shapes=[*(pltpu.VMEM((rows, column_halves(width)[-1].size), f32),) * 3, dma((9,))],
        compiler_params=pltpu.CompilerParams(vmem_limit_bytes=2**22),
    )(*outs)
    return tuple(x[None] for x in outs[:5]) + (outs[5],)


def solution(mesh):
    n, layers = mesh.shape["dp"], mesh.shape["layer"]
    body = functools.partial(gathered_body, n, layers) if n <= 8 else summed_body
    return jax.shard_map(
        body,
        mesh=mesh,
        in_specs=(
            P("layer", ("groups", "dp"), None),
            P("layer", ("groups", "dp"), None),
            P("layer", ("groups", "dp"), None),
            P("layer", ("groups", "dp"), None),
            P(("groups", "layer"), None, None),
            P(("groups", "layer"), None),
            P(("groups", "dp"), None),
            P(("groups", "dp"), None),
            P(("groups", "dp"), None),
            P(("groups", "dp"), None),
        ),
        out_specs=(
            P("layer", ("groups", "dp"), None),
            P("layer", ("groups", "dp"), None),
            P("layer", ("groups", "dp"), None),
            P("layer", ("groups", "dp"), None),
            P(("groups", "layer"), None, None),
            P(("groups", "layer"), None),
        ),
        check_vma=False,
    )
```

```python
import functools

import jax
import jax.numpy as jnp
from jax import lax
from jax.experimental import pallas as pl
from jax.experimental.pallas import tpu as pltpu
from jax.sharding import PartitionSpec as P

INNER = 3


penalty_nu = 1.0
penalty_rho = 1.0
step_input = 0.2
step_weight = 0.3
step_preact = 0.5


def from_behind(x, axis, by):
    count = lax.axis_size(axis)
    pairs = [(i, i + by) for i in range(count) if 0 <= i + by < count]
    return lax.ppermute(x, axis, pairs)


def matmul(left, right):
    return jnp.dot(left, right, precision=lax.Precision.HIGHEST)


def summed_body(
    layer_inputs,
    pre_acts,
    layer_outputs,
    multipliers,
    weights,
    biases,
    prev_outputs,
    prev_multipliers,
    next_inputs,
    row_order,
):
    row_perm = row_order[0]
    edge_outputs = jnp.take(prev_outputs, row_perm, axis=0)
    edge_duals = jnp.take(prev_multipliers, row_perm, axis=0)
    edge_inputs = jnp.take(next_inputs, row_perm, axis=0)
    first_layer = lax.axis_index("layer") == 0
    last_layer = lax.axis_index("layer") == lax.axis_size("layer") - 1
    row_count = layer_inputs.shape[1] * lax.axis_size("dp")
    scale = step_weight / row_count
    inputs, preact, outputs, duals = (
        layer_inputs[0],
        pre_acts[0],
        layer_outputs[0],
        multipliers[0],
    )
    weight, offset = (weights[0], biases[0])
    before_out, before_dual = from_behind((outputs, duals), "layer", 1)
    before_out = jnp.where(first_layer, edge_outputs, before_out)
    before_dual = jnp.where(first_layer, edge_duals, before_dual)
    coupling = before_dual + penalty_rho * (inputs - before_out)
    residual = matmul(inputs, weight) + offset[None, :] - preact
    inputs = inputs - step_input * (penalty_nu * matmul(residual, weight.T) + coupling)
    gram_matrix, cross_term, column_sums, preact_sums = lax.psum(
        (
            matmul(inputs.T, inputs),
            matmul(inputs.T, preact),
            jnp.sum(inputs, axis=0),
            jnp.sum(preact, axis=0),
        ),
        "dp",
    )
    for inner_step in range(INNER):
        grad_weight = (
            matmul(gram_matrix, weight) + column_sums[:, None] * offset[None, :] - cross_term
        )
        grad_offset = matmul(column_sums[None, :], weight)[0] + row_count * offset - preact_sums
        weight = weight - scale * grad_weight
        offset = offset - scale * grad_offset
    target = matmul(inputs, weight) + offset[None, :]
    preact = preact - step_preact * (
        preact - target + (jax.nn.softplus(preact) - outputs) * jax.nn.sigmoid(preact)
    )
    after_in = from_behind(inputs, "layer", -1)
    after_in = jnp.where(last_layer, edge_inputs, after_in)
    outputs = (penalty_nu * jax.nn.softplus(preact) + duals + penalty_rho * after_in) / (
        penalty_nu + penalty_rho
    )
    duals = duals + penalty_rho * (after_in - outputs)
    return (inputs[None], preact[None], outputs[None], duals[None], weight[None], offset[None])


MESH = pl.DeviceIdType.MESH
VMEM_BYTES = 67043328
NN = (((1,), (0,)), ((), ()))
NT = (((1,), (1,)), ((), ()))


def split(x):
    high = x.astype(jnp.bfloat16)
    return high, (x - high.astype(jnp.float32)).astype(jnp.bfloat16)


def dot3(left, right, dims=NN):
    def one(a, b):
        return lax.dot_general(a, b, dims, preferred_element_type=jnp.float32)

    return one(left[0], right[0]) + (one(left[0], right[1]) + one(left[1], right[0]))


def softplus(v):
    return jnp.maximum(v, 0.0) + jnp.log1p(jnp.exp(-jnp.abs(v)))


def permuted(order, x):
    rows = x.shape[0]
    stored = lax.broadcasted_iota(jnp.int32, (rows, rows), 0)
    pick = jnp.where(stored == order, 1.0, 0.0).T.astype(jnp.bfloat16)
    high, rest = split(x)
    rest = x - high.astype(jnp.float32)
    mid, low = split(rest)

    def one(part):
        return jnp.dot(pick, part, preferred_element_type=jnp.float32)

    return one(high) + (one(mid) + one(low))


def column_halves(width):
    return [pl.ds(0, width // 2), pl.ds(width // 2, width // 2)]


def z_pieces(rows, width):
    left, right = column_halves(width)
    some = pl.ds(0, 48 * rows // 128)
    return [(pl.ds(0, rows), left), (pl.ds(some.size, rows - some.size), right), (some, right)]


def kernel(
    n, layers,
    p_hbm, z_hbm, q_hbm, u_hbm, w_hbm, b_hbm, qb_hbm, ub_hbm, pb_hbm, order_hbm,
    p_out, z_out, q_out, u_out, w_out, b_out,
    p_ref, z_ref, q_ref, u_ref, w_ref, b_ref, qb_ref, ub_ref, pb_ref, order_ref,
    p_all, z_all, aside, coupling, p_next, own_coupling, w_hi, w_lo, p_hi, p_lo, pt_hi, pt_lo, target0, t_hi, t_lo, change, z_part, q_part,
    z_right, z_left, z_recv, p_right, p_left, p_recv, layer_send, layer_recv, loads, ready, aside_send, aside_recv,
):
    rows, width = p_ref.shape
    total = rows * n
    me, layer = lax.axis_index("dp"), lax.axis_index("layer")
    scale = step_weight / total
    has_left, has_right = me > 0, me < n - 1
    has_below, has_above = layer > 0, layer < layers - 1
    columns, parts, halves = column_halves(width), z_pieces(rows, width), p_recv.shape[1]
    pieces = len(parts)
    row_half = [pl.ds(i * (rows // halves), rows // halves) for i in range(halves)]

    middle = n // 2
    tells_right, tells_left = jnp.logical_and(has_right, me < middle), me > middle
    told_by_left, told_by_right = jnp.logical_and(has_left, me <= middle), jnp.logical_and(has_right, me >= middle)

    barrier = pltpu.get_barrier_semaphore()
    for there, axis, index in (
        (tells_right, "dp", me + 1), (tells_left, "dp", me - 1),
        (has_below, "layer", layer - 1), (has_above, "layer", layer + 1),
    ):
        @pl.when(there)
        def _():
            pl.semaphore_signal(barrier, inc=1, device_id={axis: index}, device_id_type=MESH)

    load = {}
    for i, (name, source, target) in enumerate((
        ("u", u_hbm, u_ref), ("q", q_hbm, q_ref), ("w", w_hbm, w_ref), ("p", p_hbm, p_ref), ("b", b_hbm, b_ref),
        ("z", z_hbm, z_ref), ("order", order_hbm, order_ref), ("ub", ub_hbm, ub_ref), ("qb", qb_hbm, qb_ref),
        ("pb", pb_hbm, pb_ref),
    )):
        load[name] = pltpu.make_async_copy(source, target, loads.at[i])
        load[name].start()

    def z_copy(owner, i, to_right, own=False):
        return pltpu.make_async_remote_copy(
            src_ref=(z_hbm if own else z_all.at[owner]).at[*parts[i]], dst_ref=z_all.at[owner, *parts[i]],
            send_sem=(z_right if to_right else z_left).at[owner, i], recv_sem=z_recv.at[owner, i],
            device_id={"dp": me + 1 if to_right else me - 1}, device_id_type=MESH,
        )

    def p_copy(owner, i, to_right):
        return pltpu.make_async_remote_copy(
            src_ref=p_all.at[owner, row_half[i]], dst_ref=p_all.at[owner, row_half[i]],
            send_sem=(p_right if to_right else p_left).at[owner, i], recv_sem=p_recv.at[owner, i],
            device_id={"dp": me + 1 if to_right else me - 1}, device_id_type=MESH,
        )

    up = pltpu.make_async_remote_copy(
        src_ref=own_coupling, dst_ref=coupling, send_sem=layer_send.at[0], recv_sem=layer_recv.at[0],
        device_id={"layer": layer + 1}, device_id_type=MESH,
    )
    down = pltpu.make_async_remote_copy(
        src_ref=p_all.at[me], dst_ref=p_next, send_sem=layer_send.at[1], recv_sem=layer_recv.at[1],
        device_id={"layer": layer - 1}, device_id_type=MESH,
    )

    def send(copy, indices, to_right):
        @pl.when(has_right if to_right else has_left)
        def _():
            for i in indices:
                copy(me, i, to_right).start()

    near_left = me < n // 2

    def relay(s, copy, indices, to_end=None):
        to_left, to_right = jnp.logical_and(me + s < n, has_left), jnp.logical_and(me >= s, has_right)
        if to_end is not None:
            to_left = jnp.logical_and(to_left, me == 1 if to_end else me != 1)
            to_right = jnp.logical_and(to_right, me == n - 2 if to_end else me != n - 2)

        def leftward(some):
            for i in some:
                if copy is z_copy and has_aside and s == 1 and i == turned:
                    @pl.when(jnp.logical_not(leaves))
                    def _():
                        copy(me + s, i, False).wait_recv()
                        copy(me + s, i, False).start()
                else:
                    copy(me + s, i, False).wait_recv()
                    copy(me + s, i, False).start()

        def rightward(some):
            for i in some:
                copy(me - s, i, True).wait_recv()
                copy(me - s, i, True).start()

        for some in [[i] for i in indices]:
            pl.when(jnp.logical_and(to_left, near_left))(lambda: leftward(some))
            pl.when(to_right)(lambda: rightward(some))
            pl.when(jnp.logical_and(to_left, jnp.logical_not(near_left)))(lambda: leftward(some))

    turned, way = pieces - 1, min(2, n - 1)
    has_aside = n > 2 and layers > 2
    leaves = jnp.logical_and(layer == 0, me == 1)
    passes = jnp.logical_and(layer == 2, me == 1)
    returns = jnp.logical_and(layer == 2, me == 0)
    asides = [
        pltpu.make_async_remote_copy(
            src_ref=source, dst_ref=target, send_sem=aside_send.at[0], recv_sem=received,
            device_id=there, device_id_type=MESH,
        )
        for source, target, received, there in (
            (z_all.at[way, *parts[turned]], aside, aside_recv.at[0], {"layer": layer + 2}),
            (aside, aside, aside_recv.at[1], {"dp": me - 1}),
            (aside, z_all.at[way, *parts[turned]], z_recv.at[way, turned], {"layer": layer - 2}),
        )
    ]

    def arrive(s, copy, indices):
        @pl.when(jnp.logical_and(me >= s, jnp.logical_not(has_right)))
        def _():
            for i in indices:
                copy(me - s, i, True).wait_recv()

        @pl.when(jnp.logical_and(me + s < n, jnp.logical_not(has_left)))
        def _():
            for i in indices:
                copy(me + s, i, False).wait_recv()

    def use(s, step):
        pl.when(me >= s)(lambda: step(me - s))
        pl.when(me + s < n)(lambda: step(me + s))

    ends = [jnp.where(there, 1, 0) for there in (told_by_left, told_by_right, has_below, has_above)]
    pl.semaphore_wait(barrier, ends[0] + ends[1] + ends[2] + ends[3])
    own_z = functools.partial(z_copy, own=True)

    @pl.when(told_by_left)
    def _():
        for i in range(pieces):
            own_z(me, i, False).start()
        pl.semaphore_signal(ready.at[0], inc=1, device_id={"dp": me - 1}, device_id_type=MESH)

    @pl.when(told_by_right)
    def _():
        for i in range(pieces):
            own_z(me, i, True).start()
        pl.semaphore_signal(ready.at[1], inc=1, device_id={"dp": me + 1}, device_id_type=MESH)

    load["u"].wait()
    load["q"].wait()
    own_coupling[...] = u_ref[...] - q_ref[...]
    pl.when(has_above)(lambda: up.start())

    for name in ("w", "p", "b", "z", "order", "ub", "qb", "pb"):
        load[name].wait()
    w_hi[...], w_lo[...] = split(w_ref[...])
    weight = (w_hi[...], w_lo[...])
    p, z, bias = p_ref[...], z_ref[...], b_ref[...]
    residual = dot3(split(p), weight) + bias - z

    @pl.when(tells_right)
    def _():
        pl.semaphore_wait(ready.at[0], 1)
        for i in range(pieces):
            own_z(me, i, True).start()

    @pl.when(tells_left)
    def _():
        pl.semaphore_wait(ready.at[1], 1)
        for i in range(pieces):
            own_z(me, i, False).start()

    back = dot3(split(residual), weight, NT)

    @pl.when(jnp.logical_not(has_below))
    def _():
        coupling[...] = permuted(order_ref[...], ub_ref[...] - qb_ref[...])

    pl.when(has_below)(lambda: up.wait_recv())
    p = p - step_input * (back + (coupling[...] + p))
    p_all[me] = p
    send(p_copy, range(halves), False)
    send(p_copy, range(halves), True)
    pl.when(has_below)(lambda: down.start())
    first, rest = range(1), range(1, pieces)
    relay(1, z_copy, first, True)
    p_out[...] = p

    @pl.when(jnp.logical_not(has_above))
    def _():
        p_next[...] = permuted(order_ref[...], pb_ref[...])

    pt_hi[pl.ds(width, 16), :] = jnp.ones((16, total), jnp.bfloat16)
    pt_lo[pl.ds(width, 16), :] = jnp.zeros((16, total), jnp.bfloat16)

    def block(owner):
        return pl.ds(pl.multiple_of(owner * rows, rows), rows)

    def take_p(owner):
        value = p_all[owner]
        high, low = split(value)
        p_hi[block(owner), :], p_lo[block(owner), :] = high, low
        across = split(value.T)
        pt_hi[pl.ds(0, width), block(owner)] = across[0]
        pt_lo[pl.ds(0, width), block(owner)] = across[1]
        target0[block(owner), :] = dot3((high, low), (w_hi[...], w_lo[...])) + b_ref[...]

    def take_above():
        pl.when(has_above)(lambda: down.wait_recv())
        q_part[...] = penalty_rho * p_next[...] + u_ref[...]

    take_p(me)
    z, q = z_ref[...], q_ref[...]
    target0[block(me), :] -= z
    z_part[...] = z - step_preact * (z + (softplus(z) - q) * jax.nn.sigmoid(z))
    take_above()
    if has_aside:
        @pl.when(leaves)
        def _():
            z_copy(way, turned, False).wait_recv()
            asides[0].start()

        @pl.when(passes)
        def _():
            asides[0].wait_recv()
            asides[1].start()

    for s in range(1, n):
        relay(s, p_copy, range(halves))
        if s == 1:
            relay(1, z_copy, first, False)
        if s > 1 and s < n - 1:
            relay(s - 1, z_copy, rest)
            relay(s, z_copy, first)
        arrive(s, p_copy, range(halves))
        use(s, take_p)
        if s == 1 and has_aside:
            @pl.when(returns)
            def _():
                asides[1].wait_recv()
                asides[2].start()
    if n > 2:
        relay(n - 2, z_copy, rest)

    stacked = (p_hi[...], p_lo[...])
    moment = scale * (dot3(stacked, stacked, NT) + 1.0)
    moment_parts = split(moment)
    same = lax.broadcasted_iota(jnp.int32, (total, total), 0) == lax.broadcasted_iota(jnp.int32, (total, total), 1)
    steps = jnp.where(same, 3.0, 0.0) - 3.0 * moment + dot3(moment_parts, moment_parts)
    t = scale * dot3((pt_hi[...], pt_lo[...]), split(steps))
    t_hi[...], t_lo[...] = split(t)

    def take_z(owner):
        target0[block(owner), :] -= z_all[owner]

    for s in range(1, n - 1):
        arrive(s, z_copy, range(pieces))
        use(s, take_z)
    change[...] = dot3((t_hi[...], t_lo[...]), split(target0[...]))
    if has_aside:
        for there, copy in zip((leaves, passes, returns), asides):
            pl.when(there)(lambda: copy.wait_send())
    for owner in range(n):
        @pl.when(jnp.logical_and(me >= owner, has_right))
        def _():
            for i in range(halves):
                p_copy(owner, i, True).wait_send()
        @pl.when(jnp.logical_and(me <= owner, has_left))
        def _():
            for i in range(halves):
                p_copy(owner, i, False).wait_send()
    pl.when(has_above)(lambda: up.wait_send())
    pl.when(has_below)(lambda: down.wait_send())
    p_parts = split(p_all[me])
    z_out[:, columns[-1]] = z_part[:, columns[-1]]
    q_out[:, columns[-1]] = q_part[:, columns[-1]]
    for i, some in enumerate(columns):
        def add(owner):
            change[:, some] -= dot3((t_hi[:, block(owner)], t_lo[:, block(owner)]), split(z_all[owner, :, some]))

        if n > 1:
            arrive(n - 1, z_copy, [[0], [1, 2]][i])
            use(n - 1, add)
        w = w_ref[:, some] - change[pl.ds(0, width), some]
        bias = b_ref[:, some] - change[pl.ds(width, 1), some]
        w_out[:, some] = w
        b_out[:, some] = bias
        if i == len(columns) - 1:
            break
        z = z_part[:, some] + step_preact * (dot3(p_parts, split(w)) + bias)
        z_out[:, some] = z
        known = q_part[:, some]
        q = (penalty_nu * softplus(z) + known) / (penalty_nu + penalty_rho)
        q_out[:, some] = q
        u_out[:, some] = known - penalty_rho * q

    for owner in range(n):
        @pl.when(jnp.logical_and(me >= owner, has_right))
        def _():
            for i in range(pieces):
                z_copy(owner, i, True).wait_send()
        @pl.when(jnp.logical_and(me <= owner, has_left))
        def _():
            for i in range(pieces):
                if has_aside and owner == way and i == turned:
                    pl.when(jnp.logical_not(leaves))(lambda: z_copy(owner, i, False).wait_send())
                else:
                    z_copy(owner, i, False).wait_send()


def last_kernel(
    p_ref, z_ref, q_ref, u_ref, w_ref, b_ref, p_hbm, z_hbm, q_hbm, u_hbm, w_hbm, b_hbm, z_last, q_last, u_last, sems
):
    width = p_ref.shape[1]
    last = column_halves(width)[-1]
    done = pl.ds(0, last.start)
    copies = [pltpu.make_async_copy(a, b, sems.at[i]) for i, (a, b) in enumerate((
        (w_ref, w_hbm), (p_ref, p_hbm), (b_ref, b_hbm), (z_ref.at[:, done], z_hbm.at[:, done]),
        (q_ref.at[:, done], q_hbm.at[:, done]), (u_ref.at[:, done], u_hbm.at[:, done]),
        (z_last, z_hbm.at[:, last]), (q_last, q_hbm.at[:, last]), (u_last, u_hbm.at[:, last]),
    ))]
    for copy in copies[:6]:
        copy.start()
    z = z_ref[:, last] + step_preact * (dot3(split(p_ref[...]), split(w_ref[:, last])) + b_ref[:, last])
    z_last[...] = z
    copies[6].start()
    known = q_ref[:, last]
    q = (penalty_nu * softplus(z) + known) / (penalty_nu + penalty_rho)
    q_last[...] = q
    copies[7].start()
    u_last[...] = known - penalty_rho * q
    copies[8].start()
    for copy in copies:
        copy.wait()


def gathered_body(n, layers, layer_inputs, pre_acts, layer_outputs, multipliers, weights, biases, prev_outputs, prev_multipliers, next_inputs, row_order):
    rows, width = prev_outputs.shape
    total = rows * n
    parts, halves = z_pieces(rows, width), 2
    pieces = len(parts)
    f32, b16 = jnp.float32, jnp.bfloat16
    dma = pltpu.SemaphoreType.DMA
    block = jax.ShapeDtypeStruct((rows, width), f32)
    hbm = pl.BlockSpec(memory_space=pltpu.HBM)
    shapes = (block,) * 4 + (jax.ShapeDtypeStruct((width, width), f32), jax.ShapeDtypeStruct((1, width), f32))
    vm = pl.BlockSpec(memory_space=pltpu.VMEM)
    kept = (sum(x.size for x in shapes) * 4 + 2**14) // 2**12 * 2**12
    outs = pl.pallas_call(
        functools.partial(kernel, n, layers),
        out_shape=tuple(pltpu.VMEM(x.shape, x.dtype) for x in shapes),
        in_specs=[hbm] * 10,
        out_specs=(vm,) * 6,
        scratch_shapes=[
            *(pltpu.VMEM((rows, width), f32),) * 4,
            pltpu.VMEM((width, width), f32), pltpu.VMEM((1, width), f32),
            *(pltpu.VMEM((rows, width), f32),) * 3,
            pltpu.VMEM((1, rows), jnp.int32),
            pltpu.VMEM((n, rows, width), f32), pltpu.VMEM((n, rows, width), f32), pltpu.VMEM((parts[-1][0].size, parts[-1][1].size), f32),
            pltpu.VMEM((rows, width), f32), pltpu.VMEM((rows, width), f32), pltpu.VMEM((rows, width), f32),
            pltpu.VMEM((width, width), b16), pltpu.VMEM((width, width), b16),
            pltpu.VMEM((total, width), b16), pltpu.VMEM((total, width), b16),
            pltpu.VMEM((width + 16, total), b16), pltpu.VMEM((width + 16, total), b16),
            pltpu.VMEM((total, width), f32),
            pltpu.VMEM((width + 16, total), b16), pltpu.VMEM((width + 16, total), b16),
            pltpu.VMEM((width + 16, width), f32), pltpu.VMEM((rows, width), f32), pltpu.VMEM((rows, width), f32),
            *(dma((n, pieces)),) * 3, *(dma((n, halves)),) * 3, dma((2,)), dma((2,)), dma((10,)), pltpu.SemaphoreType.REGULAR((2,)),
            dma((1,)), dma((2,)),
        ],
        compiler_params=pltpu.CompilerParams(collective_id=0, has_side_effects=True, vmem_limit_bytes=VMEM_BYTES - kept),
    )(layer_inputs[0], pre_acts[0], layer_outputs[0], multipliers[0], weights[0], biases, prev_outputs, prev_multipliers, next_inputs, row_order)
    outs = pl.pallas_call(
        last_kernel, out_shape=shapes, in_specs=[vm] * 6, out_specs=(hbm,) * 6,
        scratch_shapes=[*(pltpu.VMEM((rows, column_halves(width)[-1].size), f32),) * 3, dma((9,))],
        compiler_params=pltpu.CompilerParams(vmem_limit_bytes=2**22),
    )(*outs)
    return tuple(x[None] for x in outs[:5]) + (outs[5],)


def solution(mesh):
    n, layers = mesh.shape["dp"], mesh.shape["layer"]
    body = functools.partial(gathered_body, n, layers) if n <= 8 else summed_body
    return jax.shard_map(
        body,
        mesh=mesh,
        in_specs=(
            P("layer", ("groups", "dp"), None),
            P("layer", ("groups", "dp"), None),
            P("layer", ("groups", "dp"), None),
            P("layer", ("groups", "dp"), None),
            P(("groups", "layer"), None, None),
            P(("groups", "layer"), None),
            P(("groups", "dp"), None),
            P(("groups", "dp"), None),
            P(("groups", "dp"), None),
            P(("groups", "dp"), None),
        ),
        out_specs=(
            P("layer", ("groups", "dp"), None),
            P("layer", ("groups", "dp"), None),
            P("layer", ("groups", "dp"), None),
            P("layer", ("groups", "dp"), None),
            P(("groups", "layer"), None, None),
            P(("groups", "layer"), None),
        ),
        check_vma=False,
    )
```

```python
import functools

import jax
import jax.numpy as jnp
from jax import lax
from jax.experimental import pallas as pl
from jax.experimental.pallas import tpu as pltpu
from jax.sharding import PartitionSpec as P

INNER = 3


penalty_nu = 1.0
penalty_rho = 1.0
step_input = 0.2
step_weight = 0.3
step_preact = 0.5


def from_behind(x, axis, by):
    count = lax.axis_size(axis)
    pairs = [(i, i + by) for i in range(count) if 0 <= i + by < count]
    return lax.ppermute(x, axis, pairs)


def matmul(left, right):
    return jnp.dot(left, right, precision=lax.Precision.HIGHEST)


def summed_body(
    layer_inputs,
    pre_acts,
    layer_outputs,
    multipliers,
    weights,
    biases,
    prev_outputs,
    prev_multipliers,
    next_inputs,
    row_order,
):
    row_perm = row_order[0]
    edge_outputs = jnp.take(prev_outputs, row_perm, axis=0)
    edge_duals = jnp.take(prev_multipliers, row_perm, axis=0)
    edge_inputs = jnp.take(next_inputs, row_perm, axis=0)
    first_layer = lax.axis_index("layer") == 0
    last_layer = lax.axis_index("layer") == lax.axis_size("layer") - 1
    row_count = layer_inputs.shape[1] * lax.axis_size("dp")
    scale = step_weight / row_count
    inputs, preact, outputs, duals = (
        layer_inputs[0],
        pre_acts[0],
        layer_outputs[0],
        multipliers[0],
    )
    weight, offset = (weights[0], biases[0])
    before_out, before_dual = from_behind((outputs, duals), "layer", 1)
    before_out = jnp.where(first_layer, edge_outputs, before_out)
    before_dual = jnp.where(first_layer, edge_duals, before_dual)
    coupling = before_dual + penalty_rho * (inputs - before_out)
    residual = matmul(inputs, weight) + offset[None, :] - preact
    inputs = inputs - step_input * (penalty_nu * matmul(residual, weight.T) + coupling)
    gram_matrix, cross_term, column_sums, preact_sums = lax.psum(
        (
            matmul(inputs.T, inputs),
            matmul(inputs.T, preact),
            jnp.sum(inputs, axis=0),
            jnp.sum(preact, axis=0),
        ),
        "dp",
    )
    for inner_step in range(INNER):
        grad_weight = (
            matmul(gram_matrix, weight) + column_sums[:, None] * offset[None, :] - cross_term
        )
        grad_offset = matmul(column_sums[None, :], weight)[0] + row_count * offset - preact_sums
        weight = weight - scale * grad_weight
        offset = offset - scale * grad_offset
    target = matmul(inputs, weight) + offset[None, :]
    preact = preact - step_preact * (
        preact - target + (jax.nn.softplus(preact) - outputs) * jax.nn.sigmoid(preact)
    )
    after_in = from_behind(inputs, "layer", -1)
    after_in = jnp.where(last_layer, edge_inputs, after_in)
    outputs = (penalty_nu * jax.nn.softplus(preact) + duals + penalty_rho * after_in) / (
        penalty_nu + penalty_rho
    )
    duals = duals + penalty_rho * (after_in - outputs)
    return (inputs[None], preact[None], outputs[None], duals[None], weight[None], offset[None])


MESH = pl.DeviceIdType.MESH
VMEM_BYTES = 67043328
NN = (((1,), (0,)), ((), ()))
NT = (((1,), (1,)), ((), ()))


def split(x):
    high = x.astype(jnp.bfloat16)
    return high, (x - high.astype(jnp.float32)).astype(jnp.bfloat16)


def dot3(left, right, dims=NN):
    def one(a, b):
        return lax.dot_general(a, b, dims, preferred_element_type=jnp.float32)

    return one(left[0], right[0]) + (one(left[0], right[1]) + one(left[1], right[0]))


def softplus(v):
    return jnp.maximum(v, 0.0) + jnp.log1p(jnp.exp(-jnp.abs(v)))


def permuted(order, x):
    rows = x.shape[0]
    stored = lax.broadcasted_iota(jnp.int32, (rows, rows), 0)
    pick = jnp.where(stored == order, 1.0, 0.0).T.astype(jnp.bfloat16)
    high, rest = split(x)
    rest = x - high.astype(jnp.float32)
    mid, low = split(rest)

    def one(part):
        return jnp.dot(pick, part, preferred_element_type=jnp.float32)

    return one(high) + (one(mid) + one(low))


def column_halves(width):
    return [pl.ds(0, width // 2), pl.ds(width // 2, width // 2)]


def z_pieces(rows, width):
    left, right = column_halves(width)
    some = pl.ds(0, 48 * rows // 128)
    return [(pl.ds(0, rows), left), (pl.ds(some.size, rows - some.size), right), (some, right)]


def kernel(
    n, layers,
    p_hbm, z_hbm, q_hbm, u_hbm, w_hbm, b_hbm, qb_hbm, ub_hbm, pb_hbm, order_hbm,
    p_out, z_out, q_out, u_out, w_out, b_out,
    p_ref, z_ref, q_ref, u_ref, w_ref, b_ref, qb_ref, ub_ref, pb_ref, order_ref,
    p_all, z_all, aside, coupling, p_next, own_coupling, w_hi, w_lo, p_hi, p_lo, pt_hi, pt_lo, target0, t_hi, t_lo, change, z_part, q_part,
    sends, z_recv, p_recv, layer_send, layer_recv, loads, ready, aside_send, aside_recv,
):
    rows, width = p_ref.shape
    total = rows * n
    me, layer = lax.axis_index("dp"), lax.axis_index("layer")
    scale = step_weight / total
    has_left, has_right = me > 0, me < n - 1
    has_below, has_above = layer > 0, layer < layers - 1
    columns, parts, halves = column_halves(width), z_pieces(rows, width), p_recv.shape[1]
    row_half = [pl.ds(i * (rows // halves), rows // halves) for i in range(halves)]

    middle = n // 2
    tells_right, tells_left = jnp.logical_and(has_right, me < middle), me > middle
    told_by_left, told_by_right = jnp.logical_and(has_left, me <= middle), jnp.logical_and(has_right, me >= middle)

    barrier = pltpu.get_barrier_semaphore()
    for there, axis, index in (
        (tells_right, "dp", me + 1), (tells_left, "dp", me - 1),
        (has_below, "layer", layer - 1), (has_above, "layer", layer + 1),
    ):
        @pl.when(there)
        def _():
            pl.semaphore_signal(barrier, inc=1, device_id={axis: index}, device_id_type=MESH)

    load = {}
    for i, (name, source, target) in enumerate((
        ("u", u_hbm, u_ref), ("q", q_hbm, q_ref), ("w", w_hbm, w_ref), ("p", p_hbm, p_ref), ("b", b_hbm, b_ref),
        ("z", z_hbm, z_ref), ("order", order_hbm, order_ref), ("ub", ub_hbm, ub_ref), ("qb", qb_hbm, qb_ref),
        ("pb", pb_hbm, pb_ref),
    )):
        load[name] = pltpu.make_async_copy(source, target, loads.at[i])
        load[name].start()

    def sent(owner, to_right, own):
        return sends.at[owner if to_right or not own else n]

    def z_copies(owner, i, to_right, own=False, stay=0):
        return [
            pltpu.make_async_remote_copy(
                src_ref=(z_hbm if own else z_all.at[owner]).at[*part], dst_ref=z_all.at[owner, *part],
                send_sem=sent(owner, to_right, own), recv_sem=z_recv.at[owner, i],
                device_id={"dp": me + 1 if to_right else me - 1}, device_id_type=MESH,
            )
            for part in (parts[:1] if i == 0 else parts[1:len(parts) - stay])
        ]

    def z_arrives(owner, i):
        block = z_all.at[owner, :, columns[i]]
        pltpu.make_async_copy(block, block, z_recv.at[owner, i]).wait()

    def p_copies(owner, i, to_right, own=False):
        return [
            pltpu.make_async_remote_copy(
                src_ref=p_all.at[owner, row_half[i]], dst_ref=p_all.at[owner, row_half[i]],
                send_sem=sent(owner, to_right, own), recv_sem=p_recv.at[owner, i],
                device_id={"dp": me + 1 if to_right else me - 1}, device_id_type=MESH,
            )
        ]

    def p_arrives(owner, i):
        block = p_all.at[owner, row_half[i]]
        pltpu.make_async_copy(block, block, p_recv.at[owner, i]).wait()

    z_moves, p_moves = (z_copies, z_arrives), (p_copies, p_arrives)

    def start(copies):
        for copy in copies:
            copy.start()

    up = pltpu.make_async_remote_copy(
        src_ref=own_coupling, dst_ref=coupling, send_sem=layer_send.at[0], recv_sem=layer_recv.at[0],
        device_id={"layer": layer + 1}, device_id_type=MESH,
    )
    down = pltpu.make_async_remote_copy(
        src_ref=p_all.at[me], dst_ref=p_next, send_sem=layer_send.at[1], recv_sem=layer_recv.at[1],
        device_id={"layer": layer - 1}, device_id_type=MESH,
    )

    def send(moves, indices, to_right):
        @pl.when(has_right if to_right else has_left)
        def _():
            for i in indices:
                start(moves[0](me, i, to_right, True))

    near_left = me < n // 2

    def relay(s, moves, indices, to_end=None):
        to_left, to_right = jnp.logical_and(me + s < n, has_left), jnp.logical_and(me >= s, has_right)
        if to_end is not None:
            to_left = jnp.logical_and(to_left, me == 1 if to_end else me != 1)
            to_right = jnp.logical_and(to_right, me == n - 2 if to_end else me != n - 2)

        def leftward(i):
            moves[1](me + s, i)
            start(moves[0](me + s, i, False))

        def rightward(i):
            moves[1](me - s, i)
            start(moves[0](me - s, i, True))

        for i in indices:
            left = to_left
            if moves is z_moves and has_aside and s == 1 and i == 1:
                left = jnp.logical_and(to_left, jnp.logical_not(leaves))
            pl.when(jnp.logical_and(left, near_left))(lambda: leftward(i))
            pl.when(to_right)(lambda: rightward(i))
            pl.when(jnp.logical_and(left, jnp.logical_not(near_left)))(lambda: leftward(i))

    turned, way = parts[-1], min(2, n - 1)
    has_aside = n > 2 and layers > 2
    leaves = jnp.logical_and(layer == 0, me == 1)
    passes = jnp.logical_and(layer == 2, me == 1)
    returns = jnp.logical_and(layer == 2, me == 0)
    asides = [
        pltpu.make_async_remote_copy(
            src_ref=source, dst_ref=target, send_sem=left, recv_sem=received,
            device_id=there, device_id_type=MESH,
        )
        for source, target, left, received, there in (
            (z_all.at[way, *turned], aside, sends.at[way], aside_recv.at[0], {"layer": layer + 2}),
            (aside, aside, aside_send.at[0], aside_recv.at[1], {"dp": me - 1}),
            (aside, z_all.at[way, *turned], aside_send.at[0], z_recv.at[way, 1], {"layer": layer - 2}),
        )
    ]

    def arrive(s, moves, indices):
        @pl.when(jnp.logical_and(me >= s, jnp.logical_not(has_right)))
        def _():
            for i in indices:
                moves[1](me - s, i)

        @pl.when(jnp.logical_and(me + s < n, jnp.logical_not(has_left)))
        def _():
            for i in indices:
                moves[1](me + s, i)

    def use(s, step):
        pl.when(me >= s)(lambda: step(me - s))
        pl.when(me + s < n)(lambda: step(me + s))

    ends = [jnp.where(there, 1, 0) for there in (told_by_left, told_by_right, has_below, has_above)]
    pl.semaphore_wait(barrier, ends[0] + ends[1] + ends[2] + ends[3])

    @pl.when(told_by_left)
    def _():
        for i in range(len(columns)):
            start(z_copies(me, i, False, True))
        pl.semaphore_signal(ready.at[0], inc=1, device_id={"dp": me - 1}, device_id_type=MESH)

    @pl.when(told_by_right)
    def _():
        for i in range(len(columns)):
            start(z_copies(me, i, True, True))
        pl.semaphore_signal(ready.at[1], inc=1, device_id={"dp": me + 1}, device_id_type=MESH)

    load["u"].wait()
    load["q"].wait()
    own_coupling[...] = u_ref[...] - q_ref[...]
    pl.when(has_above)(lambda: up.start())

    for name in ("w", "p", "b", "z", "order", "ub", "qb", "pb"):
        load[name].wait()
    w_hi[...], w_lo[...] = split(w_ref[...])
    weight = (w_hi[...], w_lo[...])
    p, z, bias = p_ref[...], z_ref[...], b_ref[...]
    residual = dot3(split(p), weight) + bias - z

    @pl.when(tells_right)
    def _():
        pl.semaphore_wait(ready.at[0], 1)
        for i in range(len(columns)):
            start(z_copies(me, i, True, True))

    @pl.when(tells_left)
    def _():
        pl.semaphore_wait(ready.at[1], 1)
        for i in range(len(columns)):
            start(z_copies(me, i, False, True))

    back = dot3(split(residual), weight, NT)

    @pl.when(jnp.logical_not(has_below))
    def _():
        coupling[...] = permuted(order_ref[...], ub_ref[...] - qb_ref[...])

    pl.when(has_below)(lambda: up.wait_recv())
    p = p - step_input * (back + (coupling[...] + p))
    p_all[me] = p
    send(p_moves, range(halves), False)
    send(p_moves, range(halves), True)
    pl.when(has_below)(lambda: down.start())
    first, rest = range(1), range(1, len(columns))
    relay(1, z_moves, first, True)
    p_out[...] = p

    @pl.when(jnp.logical_not(has_above))
    def _():
        p_next[...] = permuted(order_ref[...], pb_ref[...])

    pt_hi[pl.ds(width, 16), :] = jnp.ones((16, total), jnp.bfloat16)
    pt_lo[pl.ds(width, 16), :] = jnp.zeros((16, total), jnp.bfloat16)

    def block(owner):
        return pl.ds(pl.multiple_of(owner * rows, rows), rows)

    def take_p(owner):
        value = p_all[owner]
        high, low = split(value)
        p_hi[block(owner), :], p_lo[block(owner), :] = high, low
        across = split(value.T)
        pt_hi[pl.ds(0, width), block(owner)] = across[0]
        pt_lo[pl.ds(0, width), block(owner)] = across[1]
        target0[block(owner), :] = dot3((high, low), (w_hi[...], w_lo[...])) + b_ref[...]

    def take_above():
        pl.when(has_above)(lambda: down.wait_recv())
        q_part[...] = penalty_rho * p_next[...] + u_ref[...]

    take_p(me)
    z, q = z_ref[...], q_ref[...]
    target0[block(me), :] -= z
    z_part[...] = z - step_preact * (z + (softplus(z) - q) * jax.nn.sigmoid(z))
    take_above()
    if has_aside:
        @pl.when(leaves)
        def _():
            z_arrives(way, 1)
            asides[0].start()
            start(z_copies(way, 1, False, stay=1))

        @pl.when(passes)
        def _():
            asides[0].wait_recv()
            asides[1].start()

    for s in range(1, n):
        relay(s, p_moves, range(halves))
        if s == 1:
            relay(1, z_moves, first, False)
        if s > 1 and s < n - 1:
            relay(s - 1, z_moves, rest)
            relay(s, z_moves, first)
        arrive(s, p_moves, range(halves))
        use(s, take_p)
        if s == 1 and has_aside:
            @pl.when(returns)
            def _():
                asides[1].wait_recv()
                asides[2].start()
    if n > 2:
        relay(n - 2, z_moves, rest)

    stacked = (p_hi[...], p_lo[...])
    moment = scale * (dot3(stacked, stacked, NT) + 1.0)
    moment_parts = split(moment)
    same = lax.broadcasted_iota(jnp.int32, (total, total), 0) == lax.broadcasted_iota(jnp.int32, (total, total), 1)
    steps = jnp.where(same, 3.0, 0.0) - 3.0 * moment + dot3(moment_parts, moment_parts)
    t = scale * dot3((pt_hi[...], pt_lo[...]), split(steps))
    t_hi[...], t_lo[...] = split(t)

    def take_z(owner):
        target0[block(owner), :] -= z_all[owner]

    for s in range(1, n - 1):
        arrive(s, z_moves, range(len(columns)))
        use(s, take_z)
    change[...] = dot3((t_hi[...], t_lo[...]), split(target0[...]))
    p_parts = split(p_all[me])
    z_out[:, columns[-1]] = z_part[:, columns[-1]]
    q_out[:, columns[-1]] = q_part[:, columns[-1]]
    for i, some in enumerate(columns):
        def add(owner):
            change[:, some] -= dot3((t_hi[:, block(owner)], t_lo[:, block(owner)]), split(z_all[owner, :, some]))

        if n > 1:
            arrive(n - 1, z_moves, [i])
            use(n - 1, add)
        w = w_ref[:, some] - change[pl.ds(0, width), some]
        bias = b_ref[:, some] - change[pl.ds(width, 1), some]
        w_out[:, some] = w
        b_out[:, some] = bias
        if i == len(columns) - 1:
            break
        z = z_part[:, some] + step_preact * (dot3(p_parts, split(w)) + bias)
        z_out[:, some] = z
        known = q_part[:, some]
        q = (penalty_nu * softplus(z) + known) / (penalty_nu + penalty_rho)
        q_out[:, some] = q
        u_out[:, some] = known - penalty_rho * q

    two = z_all.at[pl.ds(0, 2)]
    for owner in range(n):
        @pl.when(jnp.where(me >= owner, has_right, has_left))
        def _():
            pltpu.make_async_copy(two, two, sends.at[owner]).wait()

    @pl.when(has_left)
    def _():
        pltpu.make_async_copy(two, two, sends.at[n]).wait()

    if has_aside:
        pl.when(passes)(lambda: asides[1].wait_send())
        pl.when(returns)(lambda: asides[2].wait_send())
    pl.when(has_above)(lambda: up.wait_send())
    pl.when(has_below)(lambda: down.wait_send())


def last_kernel(
    p_ref, z_ref, q_ref, u_ref, w_ref, b_ref, p_hbm, z_hbm, q_hbm, u_hbm, w_hbm, b_hbm, z_last, q_last, u_last, sems
):
    width = p_ref.shape[1]
    last = column_halves(width)[-1]
    done = pl.ds(0, last.start)
    copies = [pltpu.make_async_copy(a, b, sems.at[i]) for i, (a, b) in enumerate((
        (w_ref, w_hbm), (p_ref, p_hbm), (b_ref, b_hbm), (z_ref.at[:, done], z_hbm.at[:, done]),
        (q_ref.at[:, done], q_hbm.at[:, done]), (u_ref.at[:, done], u_hbm.at[:, done]),
        (z_last, z_hbm.at[:, last]), (q_last, q_hbm.at[:, last]), (u_last, u_hbm.at[:, last]),
    ))]
    for copy in copies[:6]:
        copy.start()
    z = z_ref[:, last] + step_preact * (dot3(split(p_ref[...]), split(w_ref[:, last])) + b_ref[:, last])
    z_last[...] = z
    copies[6].start()
    known = q_ref[:, last]
    q = (penalty_nu * softplus(z) + known) / (penalty_nu + penalty_rho)
    q_last[...] = q
    copies[7].start()
    u_last[...] = known - penalty_rho * q
    copies[8].start()
    for copy in copies:
        copy.wait()


def gathered_body(n, layers, layer_inputs, pre_acts, layer_outputs, multipliers, weights, biases, prev_outputs, prev_multipliers, next_inputs, row_order):
    rows, width = prev_outputs.shape
    total = rows * n
    parts, halves = z_pieces(rows, width), 2
    f32, b16 = jnp.float32, jnp.bfloat16
    dma = pltpu.SemaphoreType.DMA
    block = jax.ShapeDtypeStruct((rows, width), f32)
    hbm = pl.BlockSpec(memory_space=pltpu.HBM)
    shapes = (block,) * 4 + (jax.ShapeDtypeStruct((width, width), f32), jax.ShapeDtypeStruct((1, width), f32))
    vm = pl.BlockSpec(memory_space=pltpu.VMEM)
    kept = (sum(x.size for x in shapes) * 4 + 2**14) // 2**12 * 2**12
    outs = pl.pallas_call(
        functools.partial(kernel, n, layers),
        out_shape=tuple(pltpu.VMEM(x.shape, x.dtype) for x in shapes),
        in_specs=[hbm] * 10,
        out_specs=(vm,) * 6,
        scratch_shapes=[
            *(pltpu.VMEM((rows, width), f32),) * 4,
            pltpu.VMEM((width, width), f32), pltpu.VMEM((1, width), f32),
            *(pltpu.VMEM((rows, width), f32),) * 3,
            pltpu.VMEM((1, rows), jnp.int32),
            pltpu.VMEM((n, rows, width), f32), pltpu.VMEM((n, rows, width), f32), pltpu.VMEM((parts[-1][0].size, parts[-1][1].size), f32),
            pltpu.VMEM((rows, width), f32), pltpu.VMEM((rows, width), f32), pltpu.VMEM((rows, width), f32),
            pltpu.VMEM((width, width), b16), pltpu.VMEM((width, width), b16),
            pltpu.VMEM((total, width), b16), pltpu.VMEM((total, width), b16),
            pltpu.VMEM((width + 16, total), b16), pltpu.VMEM((width + 16, total), b16),
            pltpu.VMEM((total, width), f32),
            pltpu.VMEM((width + 16, total), b16), pltpu.VMEM((width + 16, total), b16),
            pltpu.VMEM((width + 16, width), f32), pltpu.VMEM((rows, width), f32), pltpu.VMEM((rows, width), f32),
            dma((n + 1,)), dma((n, 2)), dma((n, halves)), dma((2,)), dma((2,)), dma((10,)), pltpu.SemaphoreType.REGULAR((2,)),
            dma((1,)), dma((2,)),
        ],
        compiler_params=pltpu.CompilerParams(collective_id=0, has_side_effects=True, vmem_limit_bytes=VMEM_BYTES - kept),
    )(layer_inputs[0], pre_acts[0], layer_outputs[0], multipliers[0], weights[0], biases, prev_outputs, prev_multipliers, next_inputs, row_order)
    outs = pl.pallas_call(
        last_kernel, out_shape=shapes, in_specs=[vm] * 6, out_specs=(hbm,) * 6,
        scratch_shapes=[*(pltpu.VMEM((rows, column_halves(width)[-1].size), f32),) * 3, dma((9,))],
        compiler_params=pltpu.CompilerParams(vmem_limit_bytes=2**22),
    )(*outs)
    return tuple(x[None] for x in outs[:5]) + (outs[5],)


def solution(mesh):
    n, layers = mesh.shape["dp"], mesh.shape["layer"]
    body = functools.partial(gathered_body, n, layers) if n <= 8 else summed_body
    return jax.shard_map(
        body,
        mesh=mesh,
        in_specs=(
            P("layer", ("groups", "dp"), None),
            P("layer", ("groups", "dp"), None),
            P("layer", ("groups", "dp"), None),
            P("layer", ("groups", "dp"), None),
            P(("groups", "layer"), None, None),
            P(("groups", "layer"), None),
            P(("groups", "dp"), None),
            P(("groups", "dp"), None),
            P(("groups", "dp"), None),
            P(("groups", "dp"), None),
        ),
        out_specs=(
            P("layer", ("groups", "dp"), None),
            P("layer", ("groups", "dp"), None),
            P("layer", ("groups", "dp"), None),
            P("layer", ("groups", "dp"), None),
            P(("groups", "layer"), None, None),
            P(("groups", "layer"), None),
        ),
        check_vma=False,
    )
```

```python
import functools

import jax
import jax.numpy as jnp
from jax import lax
from jax.experimental import pallas as pl
from jax.experimental.pallas import tpu as pltpu
from jax.sharding import PartitionSpec as P

INNER = 3


penalty_nu = 1.0
penalty_rho = 1.0
step_input = 0.2
step_weight = 0.3
step_preact = 0.5


def from_behind(x, axis, by):
    count = lax.axis_size(axis)
    pairs = [(i, i + by) for i in range(count) if 0 <= i + by < count]
    return lax.ppermute(x, axis, pairs)


def matmul(left, right):
    return jnp.dot(left, right, precision=lax.Precision.HIGHEST)


def summed_body(
    layer_inputs,
    pre_acts,
    layer_outputs,
    multipliers,
    weights,
    biases,
    prev_outputs,
    prev_multipliers,
    next_inputs,
    row_order,
):
    row_perm = row_order[0]
    edge_outputs = jnp.take(prev_outputs, row_perm, axis=0)
    edge_duals = jnp.take(prev_multipliers, row_perm, axis=0)
    edge_inputs = jnp.take(next_inputs, row_perm, axis=0)
    first_layer = lax.axis_index("layer") == 0
    last_layer = lax.axis_index("layer") == lax.axis_size("layer") - 1
    row_count = layer_inputs.shape[1] * lax.axis_size("dp")
    scale = step_weight / row_count
    inputs, preact, outputs, duals = (
        layer_inputs[0],
        pre_acts[0],
        layer_outputs[0],
        multipliers[0],
    )
    weight, offset = (weights[0], biases[0])
    before_out, before_dual = from_behind((outputs, duals), "layer", 1)
    before_out = jnp.where(first_layer, edge_outputs, before_out)
    before_dual = jnp.where(first_layer, edge_duals, before_dual)
    coupling = before_dual + penalty_rho * (inputs - before_out)
    residual = matmul(inputs, weight) + offset[None, :] - preact
    inputs = inputs - step_input * (penalty_nu * matmul(residual, weight.T) + coupling)
    gram_matrix, cross_term, column_sums, preact_sums = lax.psum(
        (
            matmul(inputs.T, inputs),
            matmul(inputs.T, preact),
            jnp.sum(inputs, axis=0),
            jnp.sum(preact, axis=0),
        ),
        "dp",
    )
    for inner_step in range(INNER):
        grad_weight = (
            matmul(gram_matrix, weight) + column_sums[:, None] * offset[None, :] - cross_term
        )
        grad_offset = matmul(column_sums[None, :], weight)[0] + row_count * offset - preact_sums
        weight = weight - scale * grad_weight
        offset = offset - scale * grad_offset
    target = matmul(inputs, weight) + offset[None, :]
    preact = preact - step_preact * (
        preact - target + (jax.nn.softplus(preact) - outputs) * jax.nn.sigmoid(preact)
    )
    after_in = from_behind(inputs, "layer", -1)
    after_in = jnp.where(last_layer, edge_inputs, after_in)
    outputs = (penalty_nu * jax.nn.softplus(preact) + duals + penalty_rho * after_in) / (
        penalty_nu + penalty_rho
    )
    duals = duals + penalty_rho * (after_in - outputs)
    return (inputs[None], preact[None], outputs[None], duals[None], weight[None], offset[None])


MESH = pl.DeviceIdType.MESH
VMEM_BYTES = 67043328
NN = (((1,), (0,)), ((), ()))
NT = (((1,), (1,)), ((), ()))


def split(x):
    high = x.astype(jnp.bfloat16)
    return high, (x - high.astype(jnp.float32)).astype(jnp.bfloat16)


def dot3(left, right, dims=NN):
    def one(a, b):
        return lax.dot_general(a, b, dims, preferred_element_type=jnp.float32)

    return one(left[0], right[0]) + (one(left[0], right[1]) + one(left[1], right[0]))


def softplus(v):
    return jnp.maximum(v, 0.0) + jnp.log1p(jnp.exp(-jnp.abs(v)))


def permuted(order, x):
    rows = x.shape[0]
    stored = lax.broadcasted_iota(jnp.int32, (rows, rows), 0)
    pick = jnp.where(stored == order, 1.0, 0.0).T.astype(jnp.bfloat16)
    high, rest = split(x)
    rest = x - high.astype(jnp.float32)
    mid, low = split(rest)

    def one(part):
        return jnp.dot(pick, part, preferred_element_type=jnp.float32)

    return one(high) + (one(mid) + one(low))


def column_halves(width):
    return [pl.ds(0, width // 2), pl.ds(width // 2, width // 2)]


def z_pieces(rows, width):
    left, right = column_halves(width)
    some = pl.ds(0, 48 * rows // 128)
    return [(pl.ds(0, rows), left), (pl.ds(some.size, rows - some.size), right), (some, right)]


def kernel(
    n, layers,
    p_hbm, z_hbm, q_hbm, u_hbm, w_hbm, b_hbm, qb_hbm, ub_hbm, pb_hbm, order_hbm,
    p_out, z_out, q_out, u_out, w_out, b_out,
    p_ref, z_ref, q_ref, u_ref, w_ref, b_ref, qb_ref, ub_ref, pb_ref, order_ref,
    p_all, z_all, aside, coupling, p_next, own_coupling, w_hi, w_lo, p_hi, p_lo, pt_hi, pt_lo, target0, t_hi, t_lo, z_part, q_part,
    sends, z_recv, p_recv, layer_send, layer_recv, loads, ready, aside_send, aside_recv,
):
    rows, width = p_ref.shape
    total = rows * n
    me, layer = lax.axis_index("dp"), lax.axis_index("layer")
    scale = step_weight / total
    has_left, has_right = me > 0, me < n - 1
    has_below, has_above = layer > 0, layer < layers - 1
    columns, parts, halves = column_halves(width), z_pieces(rows, width), p_recv.shape[1]
    row_half = [pl.ds(i * (rows // halves), rows // halves) for i in range(halves)]

    middle = n // 2
    tells_right, tells_left = jnp.logical_and(has_right, me < middle), me > middle
    told_by_left, told_by_right = jnp.logical_and(has_left, me <= middle), jnp.logical_and(has_right, me >= middle)

    barrier = pltpu.get_barrier_semaphore()
    for there, axis, index in (
        (tells_right, "dp", me + 1), (tells_left, "dp", me - 1),
        (has_below, "layer", layer - 1), (has_above, "layer", layer + 1),
    ):
        @pl.when(there)
        def _():
            pl.semaphore_signal(barrier, inc=1, device_id={axis: index}, device_id_type=MESH)

    two, load = z_all.at[pl.ds(0, 2)], []
    for i, source, target in (
        (0, u_hbm, u_ref), (0, q_hbm, q_ref), (3, w_hbm, w_ref), (1, p_hbm, p_ref), (4, b_hbm, b_ref),
        (1, z_hbm, z_ref), (5, order_hbm, order_ref), (2, ub_hbm, ub_ref), (2, qb_hbm, qb_ref),
        (6, pb_hbm, pb_ref),
    ):
        copy = pltpu.make_async_copy(source, target, loads.at[i])
        copy.start()
        if i > 2:
            load.append(copy)

    def sent(owner, to_right, own):
        return sends.at[owner if to_right or not own else n]

    def z_copies(owner, i, to_right, own=False, stay=0):
        return [
            pltpu.make_async_remote_copy(
                src_ref=(z_hbm if own else z_all.at[owner]).at[*part], dst_ref=z_all.at[owner, *part],
                send_sem=sent(owner, to_right, own), recv_sem=z_recv.at[owner, i],
                device_id={"dp": me + 1 if to_right else me - 1}, device_id_type=MESH,
            )
            for part in (parts[:1] if i == 0 else parts[1:len(parts) - stay])
        ]

    def z_arrives(owner, i):
        block = z_all.at[owner, :, columns[i]]
        pltpu.make_async_copy(block, block, z_recv.at[owner, i]).wait()

    def p_copies(owner, i, to_right, own=False):
        return [
            pltpu.make_async_remote_copy(
                src_ref=p_all.at[owner, row_half[i]], dst_ref=p_all.at[owner, row_half[i]],
                send_sem=sent(owner, to_right, own), recv_sem=p_recv.at[owner, i],
                device_id={"dp": me + 1 if to_right else me - 1}, device_id_type=MESH,
            )
        ]

    def p_arrives(owner, i):
        block = p_all.at[owner, row_half[i]]
        pltpu.make_async_copy(block, block, p_recv.at[owner, i]).wait()

    z_moves, p_moves = (z_copies, z_arrives), (p_copies, p_arrives)

    def start(copies):
        for copy in copies:
            copy.start()

    up = pltpu.make_async_remote_copy(
        src_ref=own_coupling, dst_ref=coupling, send_sem=layer_send.at[0], recv_sem=layer_recv.at[0],
        device_id={"layer": layer + 1}, device_id_type=MESH,
    )
    down = pltpu.make_async_remote_copy(
        src_ref=p_all.at[me], dst_ref=p_next, send_sem=layer_send.at[1], recv_sem=layer_recv.at[1],
        device_id={"layer": layer - 1}, device_id_type=MESH,
    )

    def send(moves, indices, to_right):
        @pl.when(has_right if to_right else has_left)
        def _():
            for i in indices:
                start(moves[0](me, i, to_right, True))

    near_left = me < n // 2

    def relay(s, moves, indices, to_end=None):
        to_left, to_right = jnp.logical_and(me + s < n, has_left), jnp.logical_and(me >= s, has_right)
        if to_end is not None:
            to_left = jnp.logical_and(to_left, me == 1 if to_end else me != 1)
            to_right = jnp.logical_and(to_right, me == n - 2 if to_end else me != n - 2)

        def leftward(i):
            moves[1](me + s, i)
            start(moves[0](me + s, i, False))

        def rightward(i):
            moves[1](me - s, i)
            start(moves[0](me - s, i, True))

        for i in indices:
            left = to_left
            if moves is z_moves and has_aside and s == 1 and i == 1:
                left = jnp.logical_and(to_left, jnp.logical_not(leaves))
            pl.when(jnp.logical_and(left, near_left))(lambda: leftward(i))
            pl.when(to_right)(lambda: rightward(i))
            pl.when(jnp.logical_and(left, jnp.logical_not(near_left)))(lambda: leftward(i))

    turned, way = parts[-1], min(2, n - 1)
    has_aside = n > 2 and layers > 2
    leaves = jnp.logical_and(layer == 0, me == 1)
    passes = jnp.logical_and(layer == 2, me == 1)
    returns = jnp.logical_and(layer == 2, me == 0)
    asides = [
        pltpu.make_async_remote_copy(
            src_ref=source, dst_ref=target, send_sem=left, recv_sem=received,
            device_id=there, device_id_type=MESH,
        )
        for source, target, left, received, there in (
            (z_all.at[way, *turned], aside, sends.at[way], aside_recv.at[0], {"layer": layer + 2}),
            (aside, aside, aside_send.at[0], aside_recv.at[1], {"dp": me - 1}),
            (aside, z_all.at[way, *turned], aside_send.at[0], z_recv.at[way, 1], {"layer": layer - 2}),
        )
    ]

    def arrive(s, moves, indices):
        @pl.when(jnp.logical_and(me >= s, jnp.logical_not(has_right)))
        def _():
            for i in indices:
                moves[1](me - s, i)

        @pl.when(jnp.logical_and(me + s < n, jnp.logical_not(has_left)))
        def _():
            for i in indices:
                moves[1](me + s, i)

    def use(s, step):
        pl.when(me >= s)(lambda: step(me - s))
        pl.when(me + s < n)(lambda: step(me + s))

    ends = [jnp.where(there, 1, 0) for there in (told_by_left, told_by_right, has_below, has_above)]
    pl.semaphore_wait(barrier, ends[0] + ends[1] + ends[2] + ends[3])

    @pl.when(told_by_left)
    def _():
        for i in range(len(columns)):
            start(z_copies(me, i, False, True))
        pl.semaphore_signal(ready.at[0], inc=1, device_id={"dp": me - 1}, device_id_type=MESH)

    @pl.when(told_by_right)
    def _():
        for i in range(len(columns)):
            start(z_copies(me, i, True, True))
        pl.semaphore_signal(ready.at[1], inc=1, device_id={"dp": me + 1}, device_id_type=MESH)

    pltpu.make_async_copy(two, two, loads.at[0]).wait()
    own_coupling[...] = u_ref[...] - q_ref[...]
    pl.when(has_above)(lambda: up.start())

    for i in (1, 2):
        pltpu.make_async_copy(two, two, loads.at[i]).wait()
    for copy in load:
        copy.wait()
    w_hi[...], w_lo[...] = split(w_ref[...])
    weight = (w_hi[...], w_lo[...])
    p, z, bias = p_ref[...], z_ref[...], b_ref[...]
    residual = dot3(split(p), weight) + bias - z

    @pl.when(tells_right)
    def _():
        pl.semaphore_wait(ready.at[0], 1)
        for i in range(len(columns)):
            start(z_copies(me, i, True, True))

    @pl.when(tells_left)
    def _():
        pl.semaphore_wait(ready.at[1], 1)
        for i in range(len(columns)):
            start(z_copies(me, i, False, True))

    back = dot3(split(residual), weight, NT)

    @pl.when(jnp.logical_not(has_below))
    def _():
        coupling[...] = permuted(order_ref[...], ub_ref[...] - qb_ref[...])

    pl.when(has_below)(lambda: up.wait_recv())
    p = p - step_input * (back + (coupling[...] + p))
    p_all[me] = p
    send(p_moves, range(halves), False)
    send(p_moves, range(halves), True)
    pl.when(has_below)(lambda: down.start())
    first, rest = range(1), range(1, len(columns))
    relay(1, z_moves, first, True)
    p_out[...] = p

    @pl.when(jnp.logical_not(has_above))
    def _():
        p_next[...] = permuted(order_ref[...], pb_ref[...])

    pt_hi[pl.ds(width, 16), :] = jnp.ones((16, total), jnp.bfloat16)
    pt_lo[pl.ds(width, 16), :] = jnp.zeros((16, total), jnp.bfloat16)

    def block(owner):
        return pl.ds(pl.multiple_of(owner * rows, rows), rows)

    def take_p(owner):
        value = p_all[owner]
        high, low = split(value)
        p_hi[block(owner), :], p_lo[block(owner), :] = high, low
        across = split(value.T)
        pt_hi[pl.ds(0, width), block(owner)] = across[0]
        pt_lo[pl.ds(0, width), block(owner)] = across[1]
        target0[block(owner), :] = dot3((high, low), (w_hi[...], w_lo[...])) + b_ref[...]

    def take_above():
        pl.when(has_above)(lambda: down.wait_recv())
        q_part[...] = penalty_rho * p_next[...] + u_ref[...]

    take_p(me)
    z, q = z_ref[...], q_ref[...]
    target0[block(me), :] -= z
    z_part[...] = z - step_preact * (z + (softplus(z) - q) * jax.nn.sigmoid(z))
    take_above()
    if has_aside:
        @pl.when(leaves)
        def _():
            z_arrives(way, 1)
            asides[0].start()
            start(z_copies(way, 1, False, stay=1))

        @pl.when(passes)
        def _():
            asides[0].wait_recv()
            asides[1].start()

    for s in range(1, n):
        relay(s, p_moves, range(halves))
        if s == 1:
            relay(1, z_moves, first, False)
        if s > 1 and s < n - 1:
            relay(s - 1, z_moves, rest)
            relay(s, z_moves, first)
        arrive(s, p_moves, range(halves))
        use(s, take_p)
        if s == 1 and has_aside:
            @pl.when(returns)
            def _():
                asides[1].wait_recv()
                asides[2].start()
    if n > 2:
        relay(n - 2, z_moves, rest)

    stacked = (p_hi[...], p_lo[...])
    moment = scale * (dot3(stacked, stacked, NT) + 1.0)
    moment_parts = split(moment)
    same = lax.broadcasted_iota(jnp.int32, (total, total), 0) == lax.broadcasted_iota(jnp.int32, (total, total), 1)
    steps = jnp.where(same, 3.0, 0.0) - 3.0 * moment + dot3(moment_parts, moment_parts)
    t = scale * dot3((pt_hi[...], pt_lo[...]), split(steps))
    t_hi[...], t_lo[...] = split(t)

    def take_z(owner):
        target0[block(owner), :] -= z_all[owner]

    for s in range(1, n - 1):
        arrive(s, z_moves, range(len(columns)))
        use(s, take_z)
    change = dot3((t_hi[...], t_lo[...]), split(target0[...]))
    w_out[...] = w_ref[...] - change[:width]
    b_out[...] = b_ref[...] - change[width:width + 1]
    p_parts = split(p_all[me])
    z_out[:, columns[-1]] = z_part[:, columns[-1]]
    q_out[:, columns[-1]] = q_part[:, columns[-1]]
    for i, some in enumerate(columns):
        def add(owner):
            share = dot3((t_hi[:, block(owner)], t_lo[:, block(owner)]), split(z_all[owner, :, some]))
            w_out[:, some] += share[:width]
            b_out[:, some] += share[width:width + 1]

        if n > 1:
            arrive(n - 1, z_moves, [i])
            use(n - 1, add)
        if i == len(columns) - 1:
            break
        w, bias = w_out[:, some], b_out[:, some]
        z = z_part[:, some] + step_preact * (dot3(p_parts, split(w)) + bias)
        z_out[:, some] = z
        known = q_part[:, some]
        q = (penalty_nu * softplus(z) + known) / (penalty_nu + penalty_rho)
        q_out[:, some] = q
        u_out[:, some] = known - penalty_rho * q

    for owner in range(n):
        @pl.when(jnp.where(me >= owner, has_right, has_left))
        def _():
            pltpu.make_async_copy(two, two, sends.at[owner]).wait()

    @pl.when(has_left)
    def _():
        pltpu.make_async_copy(two, two, sends.at[n]).wait()

    if has_aside:
        pl.when(passes)(lambda: asides[1].wait_send())
        pl.when(returns)(lambda: asides[2].wait_send())
    pl.when(has_above)(lambda: up.wait_send())
    pl.when(has_below)(lambda: down.wait_send())


def last_kernel(
    p_ref, z_ref, q_ref, u_ref, w_ref, b_ref, p_hbm, z_hbm, q_hbm, u_hbm, w_hbm, b_hbm, z_last, q_last, u_last, sems
):
    width = p_ref.shape[1]
    last = column_halves(width)[-1]
    done = pl.ds(0, last.start)
    copies = [pltpu.make_async_copy(a, b, sems.at[i]) for i, a, b in (
        (0, w_ref, w_hbm), (1, p_ref, p_hbm), (2, b_ref, b_hbm), (3, z_ref.at[:, done], z_hbm.at[:, done]),
        (4, q_ref.at[:, done], q_hbm.at[:, done]), (5, u_ref.at[:, done], u_hbm.at[:, done]),
        (3, z_last, z_hbm.at[:, last]), (4, q_last, q_hbm.at[:, last]), (5, u_last, u_hbm.at[:, last]),
    )]
    for copy in copies[:6]:
        copy.start()
    z = z_ref[:, last] + step_preact * (dot3(split(p_ref[...]), split(w_ref[:, last])) + b_ref[:, last])
    z_last[...] = z
    copies[6].start()
    known = q_ref[:, last]
    q = (penalty_nu * softplus(z) + known) / (penalty_nu + penalty_rho)
    q_last[...] = q
    copies[7].start()
    u_last[...] = known - penalty_rho * q
    copies[8].start()
    for copy in copies[:3]:
        copy.wait()
    for i, whole, target in ((3, z_ref, z_hbm), (4, q_ref, q_hbm), (5, u_ref, u_hbm)):
        pltpu.make_async_copy(whole, target, sems.at[i]).wait()


def gathered_body(n, layers, layer_inputs, pre_acts, layer_outputs, multipliers, weights, biases, prev_outputs, prev_multipliers, next_inputs, row_order):
    rows, width = prev_outputs.shape
    total = rows * n
    parts, halves = z_pieces(rows, width), 2
    f32, b16 = jnp.float32, jnp.bfloat16
    dma = pltpu.SemaphoreType.DMA
    block = jax.ShapeDtypeStruct((rows, width), f32)
    hbm = pl.BlockSpec(memory_space=pltpu.HBM)
    shapes = (block,) * 4 + (jax.ShapeDtypeStruct((width, width), f32), jax.ShapeDtypeStruct((1, width), f32))
    vm = pl.BlockSpec(memory_space=pltpu.VMEM)
    kept = (sum(x.size for x in shapes) * 4 + 2**14) // 2**12 * 2**12
    outs = pl.pallas_call(
        functools.partial(kernel, n, layers),
        out_shape=tuple(pltpu.VMEM(x.shape, x.dtype) for x in shapes),
        in_specs=[hbm] * 10,
        out_specs=(vm,) * 6,
        scratch_shapes=[
            *(pltpu.VMEM((rows, width), f32),) * 4,
            pltpu.VMEM((width, width), f32), pltpu.VMEM((1, width), f32),
            *(pltpu.VMEM((rows, width), f32),) * 3,
            pltpu.VMEM((1, rows), jnp.int32),
            pltpu.VMEM((n, rows, width), f32), pltpu.VMEM((n, rows, width), f32), pltpu.VMEM((parts[-1][0].size, parts[-1][1].size), f32),
            pltpu.VMEM((rows, width), f32), pltpu.VMEM((rows, width), f32), pltpu.VMEM((rows, width), f32),
            pltpu.VMEM((width, width), b16), pltpu.VMEM((width, width), b16),
            pltpu.VMEM((total, width), b16), pltpu.VMEM((total, width), b16),
            pltpu.VMEM((width + 16, total), b16), pltpu.VMEM((width + 16, total), b16),
            pltpu.VMEM((total, width), f32),
            pltpu.VMEM((width + 16, total), b16), pltpu.VMEM((width + 16, total), b16),
            pltpu.VMEM((rows, width), f32), pltpu.VMEM((rows, width), f32),
            dma((n + 1,)), dma((n, 2)), dma((n, halves)), dma((2,)), dma((2,)), dma((7,)), pltpu.SemaphoreType.REGULAR((2,)),
            dma((1,)), dma((2,)),
        ],
        compiler_params=pltpu.CompilerParams(collective_id=0, has_side_effects=True, vmem_limit_bytes=VMEM_BYTES - kept),
    )(layer_inputs[0], pre_acts[0], layer_outputs[0], multipliers[0], weights[0], biases, prev_outputs, prev_multipliers, next_inputs, row_order)
    outs = pl.pallas_call(
        last_kernel, out_shape=shapes, in_specs=[vm] * 6, out_specs=(hbm,) * 6,
        scratch_shapes=[*(pltpu.VMEM((rows, column_halves(width)[-1].size), f32),) * 3, dma((6,))],
        compiler_params=pltpu.CompilerParams(vmem_limit_bytes=2**22),
    )(*outs)
    return tuple(x[None] for x in outs[:5]) + (outs[5],)


def solution(mesh):
    n, layers = mesh.shape["dp"], mesh.shape["layer"]
    body = functools.partial(gathered_body, n, layers) if n <= 8 else summed_body
    return jax.shard_map(
        body,
        mesh=mesh,
        in_specs=(
            P("layer", ("groups", "dp"), None),
            P("layer", ("groups", "dp"), None),
            P("layer", ("groups", "dp"), None),
            P("layer", ("groups", "dp"), None),
            P(("groups", "layer"), None, None),
            P(("groups", "layer"), None),
            P(("groups", "dp"), None),
            P(("groups", "dp"), None),
            P(("groups", "dp"), None),
            P(("groups", "dp"), None),
        ),
        out_specs=(
            P("layer", ("groups", "dp"), None),
            P("layer", ("groups", "dp"), None),
            P("layer", ("groups", "dp"), None),
            P("layer", ("groups", "dp"), None),
            P(("groups", "layer"), None, None),
            P(("groups", "layer"), None),
        ),
        check_vma=False,
    )
```

```python
import functools

import jax
import jax.numpy as jnp
from jax import lax
from jax.experimental import pallas as pl
from jax.experimental.pallas import tpu as pltpu
from jax.sharding import PartitionSpec as P

INNER = 3


penalty_nu = 1.0
penalty_rho = 1.0
step_input = 0.2
step_weight = 0.3
step_preact = 0.5


def from_behind(x, axis, by):
    count = lax.axis_size(axis)
    pairs = [(i, i + by) for i in range(count) if 0 <= i + by < count]
    return lax.ppermute(x, axis, pairs)


def matmul(left, right):
    return jnp.dot(left, right, precision=lax.Precision.HIGHEST)


def summed_body(
    layer_inputs,
    pre_acts,
    layer_outputs,
    multipliers,
    weights,
    biases,
    prev_outputs,
    prev_multipliers,
    next_inputs,
    row_order,
):
    row_perm = row_order[0]
    edge_outputs = jnp.take(prev_outputs, row_perm, axis=0)
    edge_duals = jnp.take(prev_multipliers, row_perm, axis=0)
    edge_inputs = jnp.take(next_inputs, row_perm, axis=0)
    first_layer = lax.axis_index("layer") == 0
    last_layer = lax.axis_index("layer") == lax.axis_size("layer") - 1
    row_count = layer_inputs.shape[1] * lax.axis_size("dp")
    scale = step_weight / row_count
    inputs, preact, outputs, duals = (
        layer_inputs[0],
        pre_acts[0],
        layer_outputs[0],
        multipliers[0],
    )
    weight, offset = (weights[0], biases[0])
    before_out, before_dual = from_behind((outputs, duals), "layer", 1)
    before_out = jnp.where(first_layer, edge_outputs, before_out)
    before_dual = jnp.where(first_layer, edge_duals, before_dual)
    coupling = before_dual + penalty_rho * (inputs - before_out)
    residual = matmul(inputs, weight) + offset[None, :] - preact
    inputs = inputs - step_input * (penalty_nu * matmul(residual, weight.T) + coupling)
    gram_matrix, cross_term, column_sums, preact_sums = lax.psum(
        (
            matmul(inputs.T, inputs),
            matmul(inputs.T, preact),
            jnp.sum(inputs, axis=0),
            jnp.sum(preact, axis=0),
        ),
        "dp",
    )
    for inner_step in range(INNER):
        grad_weight = (
            matmul(gram_matrix, weight) + column_sums[:, None] * offset[None, :] - cross_term
        )
        grad_offset = matmul(column_sums[None, :], weight)[0] + row_count * offset - preact_sums
        weight = weight - scale * grad_weight
        offset = offset - scale * grad_offset
    target = matmul(inputs, weight) + offset[None, :]
    preact = preact - step_preact * (
        preact - target + (jax.nn.softplus(preact) - outputs) * jax.nn.sigmoid(preact)
    )
    after_in = from_behind(inputs, "layer", -1)
    after_in = jnp.where(last_layer, edge_inputs, after_in)
    outputs = (penalty_nu * jax.nn.softplus(preact) + duals + penalty_rho * after_in) / (
        penalty_nu + penalty_rho
    )
    duals = duals + penalty_rho * (after_in - outputs)
    return (inputs[None], preact[None], outputs[None], duals[None], weight[None], offset[None])


MESH = pl.DeviceIdType.MESH
VMEM_BYTES = 67043328
NN = (((1,), (0,)), ((), ()))
NT = (((1,), (1,)), ((), ()))


def split(x):
    high = x.astype(jnp.bfloat16)
    return high, (x - high.astype(jnp.float32)).astype(jnp.bfloat16)


def dot3(left, right, dims=NN):
    def one(a, b):
        return lax.dot_general(a, b, dims, preferred_element_type=jnp.float32)

    return one(left[0], right[0]) + (one(left[0], right[1]) + one(left[1], right[0]))


def softplus(v):
    return jnp.maximum(v, 0.0) + jnp.log1p(jnp.exp(-jnp.abs(v)))


def permuted(order, x):
    rows = x.shape[0]
    stored = lax.broadcasted_iota(jnp.int32, (rows, rows), 0)
    pick = jnp.where(stored == order, 1.0, 0.0).T.astype(jnp.bfloat16)
    high, rest = split(x)
    rest = x - high.astype(jnp.float32)
    mid, low = split(rest)

    def one(part):
        return jnp.dot(pick, part, preferred_element_type=jnp.float32)

    return one(high) + (one(mid) + one(low))


def column_halves(width):
    return [pl.ds(0, width // 2), pl.ds(width // 2, width // 2)]


def z_pieces(rows, width):
    left, right = column_halves(width)
    some = pl.ds(0, 48 * rows // 128)
    return [(pl.ds(0, rows), left), (pl.ds(some.size, rows - some.size), right), (some, right)]


def kernel(
    n, layers,
    p_hbm, z_hbm, q_hbm, u_hbm, w_hbm, b_hbm, qb_hbm, ub_hbm, pb_hbm, order_hbm,
    p_out, z_out, q_out, u_out, w_out, b_out,
    p_ref, z_ref, q_ref, u_ref, w_ref, b_ref, qb_ref, ub_ref, pb_ref, order_ref,
    p_all, z_all, aside, coupling, p_next, own_coupling, w_hi, w_lo, p_hi, p_lo, pt_hi, pt_lo, target0, t_hi, t_lo, z_part, q_part,
    sends, z_recv, p_recv, layer_send, layer_recv, loads, ready, aside_send, aside_recv,
):
    rows, width = p_ref.shape
    total = rows * n
    me, layer = lax.axis_index("dp"), lax.axis_index("layer")
    scale = step_weight / total
    has_left, has_right = me > 0, me < n - 1
    has_below, has_above = layer > 0, layer < layers - 1
    columns, parts, halves = column_halves(width), z_pieces(rows, width), p_recv.shape[1]
    row_half = [pl.ds(i * (rows // halves), rows // halves) for i in range(halves)]

    middle = n // 2
    tells_right, tells_left = jnp.logical_and(has_right, me < middle), me > middle
    told_by_left, told_by_right = jnp.logical_and(has_left, me <= middle), jnp.logical_and(has_right, me >= middle)

    barrier = pltpu.get_barrier_semaphore()
    for there, axis, index in (
        (tells_right, "dp", me + 1), (tells_left, "dp", me - 1),
        (has_below, "layer", layer - 1), (has_above, "layer", layer + 1),
    ):
        @pl.when(there)
        def _():
            pl.semaphore_signal(barrier, inc=1, device_id={axis: index}, device_id_type=MESH)

    two, load = z_all.at[pl.ds(0, 2)], []
    for i, source, target in (
        (0, u_hbm, u_ref), (0, q_hbm, q_ref), (3, w_hbm, w_ref), (1, p_hbm, p_ref), (4, b_hbm, b_ref),
        (1, z_hbm, z_ref), (5, order_hbm, order_ref), (2, ub_hbm, ub_ref), (2, qb_hbm, qb_ref),
        (6, pb_hbm, pb_ref),
    ):
        copy = pltpu.make_async_copy(source, target, loads.at[i])
        copy.start()
        if i > 2:
            load.append(copy)

    def sent(owner, to_right, own):
        return sends.at[owner if to_right or not own else n]

    def z_copies(owner, i, to_right, own=False, stay=0):
        return [
            pltpu.make_async_remote_copy(
                src_ref=(z_hbm if own else z_all.at[owner]).at[*part], dst_ref=z_all.at[owner, *part],
                send_sem=sent(owner, to_right, own), recv_sem=z_recv.at[owner, i],
                device_id={"dp": me + 1 if to_right else me - 1}, device_id_type=MESH,
            )
            for part in ([parts[1]] if stay else [(pl.ds(0, rows), columns[i])])
        ]

    def z_arrives(owner, i):
        block = z_all.at[owner, :, columns[i]]
        pltpu.make_async_copy(block, block, z_recv.at[owner, i]).wait()

    def p_copies(owner, i, to_right, own=False):
        return [
            pltpu.make_async_remote_copy(
                src_ref=p_all.at[owner, row_half[i]], dst_ref=p_all.at[owner, row_half[i]],
                send_sem=sent(owner, to_right, own), recv_sem=p_recv.at[owner, i],
                device_id={"dp": me + 1 if to_right else me - 1}, device_id_type=MESH,
            )
        ]

    def p_arrives(owner, i):
        block = p_all.at[owner, row_half[i]]
        pltpu.make_async_copy(block, block, p_recv.at[owner, i]).wait()

    z_moves, p_moves = (z_copies, z_arrives), (p_copies, p_arrives)

    def start(copies):
        for copy in copies:
            copy.start()

    up = pltpu.make_async_remote_copy(
        src_ref=own_coupling, dst_ref=coupling, send_sem=layer_send.at[0], recv_sem=layer_recv.at[0],
        device_id={"layer": layer + 1}, device_id_type=MESH,
    )
    down = pltpu.make_async_remote_copy(
        src_ref=p_all.at[me], dst_ref=p_next, send_sem=layer_send.at[1], recv_sem=layer_recv.at[1],
        device_id={"layer": layer - 1}, device_id_type=MESH,
    )

    def send(moves, indices, to_right):
        @pl.when(has_right if to_right else has_left)
        def _():
            for i in indices:
                start(moves[0](me, i, to_right, True))

    near_left = me < n // 2

    def relay(s, moves, indices, to_end=None):
        to_left, to_right = jnp.logical_and(me + s < n, has_left), jnp.logical_and(me >= s, has_right)
        if to_end is not None:
            to_left = jnp.logical_and(to_left, me == 1 if to_end else me != 1)
            to_right = jnp.logical_and(to_right, me == n - 2 if to_end else me != n - 2)

        def leftward(i):
            moves[1](me + s, i)
            start(moves[0](me + s, i, False))

        def rightward(i):
            moves[1](me - s, i)
            start(moves[0](me - s, i, True))

        for i in indices:
            left = to_left
            if moves is z_moves and has_aside and s == 1 and i == 1:
                left = jnp.logical_and(to_left, jnp.logical_not(leaves))
            pl.when(jnp.logical_and(left, near_left))(lambda: leftward(i))
            pl.when(to_right)(lambda: rightward(i))
            pl.when(jnp.logical_and(left, jnp.logical_not(near_left)))(lambda: leftward(i))

    turned, way = parts[-1], min(2, n - 1)
    has_aside = n > 2 and layers > 2
    leaves = jnp.logical_and(layer == 0, me == 1)
    passes = jnp.logical_and(layer == 2, me == 1)
    returns = jnp.logical_and(layer == 2, me == 0)
    asides = [
        pltpu.make_async_remote_copy(
            src_ref=source, dst_ref=target, send_sem=left, recv_sem=received,
            device_id=there, device_id_type=MESH,
        )
        for source, target, left, received, there in (
            (z_all.at[way, *turned], aside, sends.at[way], aside_recv.at[0], {"layer": layer + 2}),
            (aside, aside, aside_send.at[0], aside_recv.at[1], {"dp": me - 1}),
            (aside, z_all.at[way, *turned], aside_send.at[0], z_recv.at[way, 1], {"layer": layer - 2}),
        )
    ]

    def arrive(s, moves, indices):
        @pl.when(jnp.logical_and(me >= s, jnp.logical_not(has_right)))
        def _():
            for i in indices:
                moves[1](me - s, i)

        @pl.when(jnp.logical_and(me + s < n, jnp.logical_not(has_left)))
        def _():
            for i in indices:
                moves[1](me + s, i)

    def use(s, step):
        pl.when(me >= s)(lambda: step(me - s))
        pl.when(me + s < n)(lambda: step(me + s))

    ends = [jnp.where(there, 1, 0) for there in (told_by_left, told_by_right, has_below, has_above)]
    pl.semaphore_wait(barrier, ends[0] + ends[1] + ends[2] + ends[3])

    @pl.when(told_by_left)
    def _():
        for i in range(len(columns)):
            start(z_copies(me, i, False, True))
        pl.semaphore_signal(ready.at[0], inc=1, device_id={"dp": me - 1}, device_id_type=MESH)

    @pl.when(told_by_right)
    def _():
        for i in range(len(columns)):
            start(z_copies(me, i, True, True))
        pl.semaphore_signal(ready.at[1], inc=1, device_id={"dp": me + 1}, device_id_type=MESH)

    pltpu.make_async_copy(two, two, loads.at[0]).wait()
    own_coupling[...] = u_ref[...] - q_ref[...]
    pl.when(has_above)(lambda: up.start())

    for i in (1, 2):
        pltpu.make_async_copy(two, two, loads.at[i]).wait()
    for copy in load:
        copy.wait()
    w_hi[...], w_lo[...] = split(w_ref[...])
    weight = (w_hi[...], w_lo[...])
    p, z, bias = p_ref[...], z_ref[...], b_ref[...]
    residual = dot3(split(p), weight) + bias - z

    @pl.when(tells_right)
    def _():
        pl.semaphore_wait(ready.at[0], 1)
        for i in range(len(columns)):
            start(z_copies(me, i, True, True))

    @pl.when(tells_left)
    def _():
        pl.semaphore_wait(ready.at[1], 1)
        for i in range(len(columns)):
            start(z_copies(me, i, False, True))

    back = dot3(split(residual), weight, NT)

    @pl.when(jnp.logical_not(has_below))
    def _():
        coupling[...] = permuted(order_ref[...], ub_ref[...] - qb_ref[...])

    pl.when(has_below)(lambda: up.wait_recv())
    p = p - step_input * (back + (coupling[...] + p))
    p_all[me] = p
    send(p_moves, range(halves), False)
    send(p_moves, range(halves), True)
    pl.when(has_below)(lambda: down.start())
    first, rest = range(1), range(1, len(columns))
    relay(1, z_moves, first, True)
    p_out[...] = p

    @pl.when(jnp.logical_not(has_above))
    def _():
        p_next[...] = permuted(order_ref[...], pb_ref[...])

    pt_hi[pl.ds(width, 16), :] = jnp.ones((16, total), jnp.bfloat16)
    pt_lo[pl.ds(width, 16), :] = jnp.zeros((16, total), jnp.bfloat16)

    def block(owner):
        return pl.ds(pl.multiple_of(owner * rows, rows), rows)

    def take_p(owner):
        value = p_all[owner]
        high, low = split(value)
        p_hi[block(owner), :], p_lo[block(owner), :] = high, low
        across = split(value.T)
        pt_hi[pl.ds(0, width), block(owner)] = across[0]
        pt_lo[pl.ds(0, width), block(owner)] = across[1]
        target0[block(owner), :] = dot3((high, low), (w_hi[...], w_lo[...])) + b_ref[...]

    def take_above():
        pl.when(has_above)(lambda: down.wait_recv())
        q_part[...] = penalty_rho * p_next[...] + u_ref[...]

    take_p(me)
    z, q = z_ref[...], q_ref[...]
    target0[block(me), :] -= z
    z_part[...] = z - step_preact * (z + (softplus(z) - q) * jax.nn.sigmoid(z))
    take_above()
    if has_aside:
        @pl.when(leaves)
        def _():
            z_arrives(way, 1)
            asides[0].start()
            start(z_copies(way, 1, False, stay=1))

        @pl.when(passes)
        def _():
            asides[0].wait_recv()
            asides[1].start()

    for s in range(1, n):
        relay(s, p_moves, range(halves))
        if s == 1:
            relay(1, z_moves, first, False)
        if s > 1 and s < n - 1:
            relay(s - 1, z_moves, rest)
            relay(s, z_moves, first)
        arrive(s, p_moves, range(halves))
        use(s, take_p)
        if s == 1 and has_aside:
            @pl.when(returns)
            def _():
                asides[1].wait_recv()
                asides[2].start()
    if n > 2:
        relay(n - 2, z_moves, rest)

    stacked = (p_hi[...], p_lo[...])
    moment = scale * (dot3(stacked, stacked, NT) + 1.0)
    moment_parts = split(moment)
    same = lax.broadcasted_iota(jnp.int32, (total, total), 0) == lax.broadcasted_iota(jnp.int32, (total, total), 1)
    steps = jnp.where(same, 3.0, 0.0) - 3.0 * moment + dot3(moment_parts, moment_parts)
    t = scale * dot3((pt_hi[...], pt_lo[...]), split(steps))
    t_hi[...], t_lo[...] = split(t)

    def take_z(owner):
        target0[block(owner), :] -= z_all[owner]

    for s in range(1, n - 1):
        arrive(s, z_moves, range(len(columns)))
        use(s, take_z)
    change = dot3((t_hi[...], t_lo[...]), split(target0[...]))
    w_out[...] = w_ref[...] - change[:width]
    b_out[...] = b_ref[...] - change[width:width + 1]
    p_parts = split(p_all[me])
    z_out[:, columns[-1]] = z_part[:, columns[-1]]
    q_out[:, columns[-1]] = q_part[:, columns[-1]]
    for i, some in enumerate(columns):
        def add(owner):
            share = dot3((t_hi[:, block(owner)], t_lo[:, block(owner)]), split(z_all[owner, :, some]))
            w_out[:, some] += share[:width]
            b_out[:, some] += share[width:width + 1]

        if n > 1:
            arrive(n - 1, z_moves, [i])
            use(n - 1, add)
        if i == len(columns) - 1:
            break
        w, bias = w_out[:, some], b_out[:, some]
        z = z_part[:, some] + step_preact * (dot3(p_parts, split(w)) + bias)
        z_out[:, some] = z
        known = q_part[:, some]
        q = (penalty_nu * softplus(z) + known) / (penalty_nu + penalty_rho)
        q_out[:, some] = q
        u_out[:, some] = known - penalty_rho * q

    for owner in range(n):
        @pl.when(jnp.where(me >= owner, has_right, has_left))
        def _():
            pltpu.make_async_copy(two, two, sends.at[owner]).wait()

    @pl.when(has_left)
    def _():
        pltpu.make_async_copy(two, two, sends.at[n]).wait()

    if has_aside:
        pl.when(passes)(lambda: asides[1].wait_send())
        pl.when(returns)(lambda: asides[2].wait_send())
    pl.when(has_above)(lambda: up.wait_send())
    pl.when(has_below)(lambda: down.wait_send())


def last_kernel(
    p_ref, z_ref, q_ref, u_ref, w_ref, b_ref, p_hbm, z_hbm, q_hbm, u_hbm, w_hbm, b_hbm, z_last, q_last, u_last, sems
):
    width = p_ref.shape[1]
    last = column_halves(width)[-1]
    done = pl.ds(0, last.start)
    copies = [pltpu.make_async_copy(a, b, sems.at[i]) for i, a, b in (
        (0, w_ref, w_hbm), (1, p_ref, p_hbm), (2, b_ref, b_hbm), (3, z_ref.at[:, done], z_hbm.at[:, done]),
        (4, q_ref.at[:, done], q_hbm.at[:, done]), (5, u_ref.at[:, done], u_hbm.at[:, done]),
        (3, z_last, z_hbm.at[:, last]), (4, q_last, q_hbm.at[:, last]), (5, u_last, u_hbm.at[:, last]),
    )]
    for copy in copies[:6]:
        copy.start()
    z = z_ref[:, last] + step_preact * (dot3(split(p_ref[...]), split(w_ref[:, last])) + b_ref[:, last])
    z_last[...] = z
    copies[6].start()
    known = q_ref[:, last]
    q = (penalty_nu * softplus(z) + known) / (penalty_nu + penalty_rho)
    q_last[...] = q
    copies[7].start()
    u_last[...] = known - penalty_rho * q
    copies[8].start()
    for copy in copies[:3]:
        copy.wait()
    for i, whole, target in ((3, z_ref, z_hbm), (4, q_ref, q_hbm), (5, u_ref, u_hbm)):
        pltpu.make_async_copy(whole, target, sems.at[i]).wait()


def gathered_body(n, layers, layer_inputs, pre_acts, layer_outputs, multipliers, weights, biases, prev_outputs, prev_multipliers, next_inputs, row_order):
    rows, width = prev_outputs.shape
    total = rows * n
    parts, halves = z_pieces(rows, width), 2
    f32, b16 = jnp.float32, jnp.bfloat16
    dma = pltpu.SemaphoreType.DMA
    block = jax.ShapeDtypeStruct((rows, width), f32)
    hbm = pl.BlockSpec(memory_space=pltpu.HBM)
    shapes = (block,) * 4 + (jax.ShapeDtypeStruct((width, width), f32), jax.ShapeDtypeStruct((1, width), f32))
    vm = pl.BlockSpec(memory_space=pltpu.VMEM)
    kept = (sum(x.size for x in shapes) * 4 + 2**14) // 2**12 * 2**12
    outs = pl.pallas_call(
        functools.partial(kernel, n, layers),
        out_shape=tuple(pltpu.VMEM(x.shape, x.dtype) for x in shapes),
        in_specs=[hbm] * 10,
        out_specs=(vm,) * 6,
        scratch_shapes=[
            *(pltpu.VMEM((rows, width), f32),) * 4,
            pltpu.VMEM((width, width), f32), pltpu.VMEM((1, width), f32),
            *(pltpu.VMEM((rows, width), f32),) * 3,
            pltpu.VMEM((1, rows), jnp.int32),
            pltpu.VMEM((n, rows, width), f32), pltpu.VMEM((n, rows, width), f32), pltpu.VMEM((parts[-1][0].size, parts[-1][1].size), f32),
            pltpu.VMEM((rows, width), f32), pltpu.VMEM((rows, width), f32), pltpu.VMEM((rows, width), f32),
            pltpu.VMEM((width, width), b16), pltpu.VMEM((width, width), b16),
            pltpu.VMEM((total, width), b16), pltpu.VMEM((total, width), b16),
            pltpu.VMEM((width + 16, total), b16), pltpu.VMEM((width + 16, total), b16),
            pltpu.VMEM((total, width), f32),
            pltpu.VMEM((width + 16, total), b16), pltpu.VMEM((width + 16, total), b16),
            pltpu.VMEM((rows, width), f32), pltpu.VMEM((rows, width), f32),
            dma((n + 1,)), dma((n, 2)), dma((n, halves)), dma((2,)), dma((2,)), dma((7,)), pltpu.SemaphoreType.REGULAR((2,)),
            dma((1,)), dma((2,)),
        ],
        compiler_params=pltpu.CompilerParams(collective_id=0, has_side_effects=True, vmem_limit_bytes=VMEM_BYTES - kept),
    )(layer_inputs[0], pre_acts[0], layer_outputs[0], multipliers[0], weights[0], biases, prev_outputs, prev_multipliers, next_inputs, row_order)
    outs = pl.pallas_call(
        last_kernel, out_shape=shapes, in_specs=[vm] * 6, out_specs=(hbm,) * 6,
        scratch_shapes=[*(pltpu.VMEM((rows, column_halves(width)[-1].size), f32),) * 3, dma((6,))],
        compiler_params=pltpu.CompilerParams(vmem_limit_bytes=2**22),
    )(*outs)
    return tuple(x[None] for x in outs[:5]) + (outs[5],)


def solution(mesh):
    n, layers = mesh.shape["dp"], mesh.shape["layer"]
    body = functools.partial(gathered_body, n, layers) if n <= 8 else summed_body
    return jax.shard_map(
        body,
        mesh=mesh,
        in_specs=(
            P("layer", ("groups", "dp"), None),
            P("layer", ("groups", "dp"), None),
            P("layer", ("groups", "dp"), None),
            P("layer", ("groups", "dp"), None),
            P(("groups", "layer"), None, None),
            P(("groups", "layer"), None),
            P(("groups", "dp"), None),
            P(("groups", "dp"), None),
            P(("groups", "dp"), None),
            P(("groups", "dp"), None),
        ),
        out_specs=(
            P("layer", ("groups", "dp"), None),
            P("layer", ("groups", "dp"), None),
            P("layer", ("groups", "dp"), None),
            P("layer", ("groups", "dp"), None),
            P(("groups", "layer"), None, None),
            P(("groups", "layer"), None),
        ),
        check_vma=False,
    )
```
